32 devices in a mesh: section: 2 (over y), wide: 8 (over z, core), narrow: 2 (over x).
Axes of the slice: x: 2, y: 2, z: 4, core: 2. Of those that a mesh axis runs over, the one named last changes fastest.
Arguments:
- hidden: bfloat16 [2, 1024, 24576], P('section', None, 'wide'), may hold values from -6 to 6
- down_weight: bfloat16 [12288, 24576], P('narrow', 'wide'), may hold values from -0.0390625 to 0.0390625
- residual: bfloat16 [2, 1024, 12288], P('section', None, 'narrow'), may hold values from -6 to 6
- ln_gain: float32 [12288], P('narrow'), may hold values from 0.5 to 1.5
- ln_bias: float32 [12288], P('narrow'), may hold values from -3 to 3
- qkv_weight: bfloat16 [12288, 24576], P('narrow', 'wide'), may hold values from -1 to 1
Outputs:
- stream: bfloat16 [2, 1024, 12288], P('section', 'wide', 'narrow')
- context: bfloat16 [2, 1024, 8192], P('section', 'narrow', 'wide')
The draws below stay inside these ranges and needn't reach their ends.
All inputs are finite; a program needn't handle non-finite values.
Results may differ from the reference program's by a relative error of at most 0.007.
Values may be sent and summed in bfloat16 or wider, within the bound.
A program may use at most 320 MiB of HBM per device.

```python
import math
import jax
import jax.numpy as jnp
from jax import lax

D = 12288
FF = 24576
HEADS = 64
HDIM = 128
SEQ = 1024
N_SECTION = 2


def column_scale(low, high):
    ramp = jnp.arange(D, dtype=jnp.float32) / jnp.float32(max(D - 1, 1))
    return jnp.exp(jnp.float32(math.log(low)) + jnp.float32(math.log(high / low)) * ramp)


def draw_residual(key, part):
    fourth = jax.random.fold_in(jax.random.fold_in(key, 11), 3)
    result = jax.random.truncated_normal(fourth, -2.0, 2.0, (2, SEQ, D), jnp.float32) * column_scale(0.5, 3.0)[None, None, :]
    return result.astype(jnp.bfloat16)


def draw_qkv_weight(key, part):
    fourth = jax.random.fold_in(jax.random.fold_in(key, 23), 3)
    scale = jnp.float32(1.0 / math.sqrt(D))
    result = jax.random.truncated_normal(fourth, -6.0, 6.0, (D, 3 * HEADS * HDIM), jnp.float32) * scale
    return result.astype(jnp.bfloat16)


def with_spikes(array, own_key, source, target, blocks, factor):
    owner, partner = [(jnp.arange(array.shape[axis_at]) // (array.shape[axis_at] // blocks)).reshape([-1 if axis == axis_at else 1 for axis in range(array.ndim)]) for axis_at in (source, target)]
    chosen = jax.random.permutation(own_key, blocks)[partner]
    strong = (owner == chosen) | (owner == (partner + blocks // 2) % blocks)
    return jnp.where(strong, factor * array, array)


def steps_of(own_key, extent, cuts, smallest, largest):
    gain, own = 1.0, jax.random.fold_in(own_key, 6)
    for axis_at, shards_of in cuts:
        draws = jnp.exp(jax.random.uniform(jax.random.fold_in(own, axis_at), (shards_of,), jnp.float32, smallest / len(cuts), largest / len(cuts)))
        gain = gain * jnp.repeat(draws, extent[axis_at] // shards_of).reshape([-1 if axis == axis_at else 1 for axis in range(len(extent))])
    return gain


def centred(stream_key, dims, deviation, most, shards=(), held_as=jnp.bfloat16):
    factor_of = steps_of(stream_key, dims, shards, -0.22, 0.18) if shards else 1.0
    values = jax.random.normal(stream_key, dims, jnp.float32) * deviation * factor_of
    return jnp.minimum(jnp.maximum(values, -most), most).astype(held_as)


def noise_with(key, shape, spread, most, shards, heavy, kind=jnp.bfloat16):
    values = spread * jax.random.normal(key, shape, jnp.float32)
    if shards:
        values = values * steps_of(key, shape, shards, -0.22, 0.18)
    return jnp.clip(with_spikes(values, jax.random.fold_in(key, 3), *heavy), -most, most).astype(kind)


def setup_inputs(seed: int = 0) -> dict:
    streams_of = jax.random.split(jax.random.key(seed), 7)
    hidden = noise_with(streams_of[0], (N_SECTION, SEQ, FF), 1.0, 6.0, ((0, 2), (2, 8)), (2, 1, 8, 2.0))
    down_weight = centred(streams_of[1], (D, FF), FF ** -0.5, 0.0390625, ((0, 2), (1, 8)))
    residual = draw_residual(jax.random.fold_in(streams_of[6], 71), 0)
    ln_gain = jnp.clip(0.5 + 1.0 * jax.random.uniform(streams_of[3], (D,), jnp.float32) ** steps_of(streams_of[3], (D,), ((0, 2),), -0.2, 0.2), 0.5, 1.5)
    ln_bias = centred(streams_of[4], (D,), 0.5, 3.0, ((0, 2),), jnp.float32)
    qkv_weight = draw_qkv_weight(jax.random.fold_in(streams_of[6], 71), 0)
    return dict(hidden=hidden, down_weight=down_weight, residual=residual, ln_gain=ln_gain, ln_bias=ln_bias, qkv_weight=qkv_weight)


def attend(joined):
    parts = joined.reshape(SEQ, HEADS, 3, HDIM).astype(jnp.float32)
    query = parts[:, :, 0]
    keys = parts[:, :, 1]
    values = parts[:, :, 2]
    scores = jnp.einsum('qhd,khd->hqk', query, keys) / jnp.sqrt(jnp.float32(HDIM))
    rows = jnp.arange(SEQ)[:, None]
    cols = jnp.arange(SEQ)[None, :]
    scores = jnp.where((cols <= rows)[None], scores, jnp.float32(-1e+30))
    top = lax.optimization_barrier(jnp.max(scores, axis=2, keepdims=True))
    expd = jnp.exp(scores - top)
    probs = (expd / lax.optimization_barrier(jnp.sum(expd, axis=2, keepdims=True))).astype(jnp.bfloat16)
    out = jnp.einsum('hqk,khd->qhd', probs.astype(jnp.float32), values)
    return out.astype(jnp.bfloat16).reshape(SEQ, HEADS * HDIM)

def reference(hidden, down_weight, residual, ln_gain, ln_bias, qkv_weight):
    streams = []
    attended = []
    for micro in range(2):
        ffn = jnp.dot(hidden[micro], down_weight.T, preferred_element_type=jnp.float32)
        stream = (residual[micro].astype(jnp.float32) + ffn).astype(jnp.bfloat16)
        values = stream.astype(jnp.float32)
        mean = lax.optimization_barrier(jnp.sum(values, axis=1)) / D
        var = lax.optimization_barrier(jnp.sum(values * values, axis=1)) / D - mean * mean
        normed = ((values - mean[:, None]) * lax.rsqrt(var + 1e-05)[:, None] * ln_gain + ln_bias).astype(jnp.bfloat16)
        joined = jnp.dot(normed, qkv_weight, preferred_element_type=jnp.float32).astype(jnp.bfloat16)
        streams.append(stream)
        attended.append(attend(joined))
    return (jnp.stack(streams), jnp.stack([attended[1], attended[0]]))
```

```python
import functools

import jax
import jax.numpy as jnp
from jax import lax
from jax.experimental import pallas as pl
from jax.experimental.pallas import tpu as pltpu
from jax.sharding import PartitionSpec as P

D = 12288
HDIM = 128
QBLOCK = 256
LANES = 128
PLACES = 4
FFN_STEPS = 24
PIECES = 6
LAG = 2
CROSS_LAG = 2
TAKE_LAG = 3
MESH = pl.DeviceIdType.MESH


def from_behind(value, axis, steps):
    count = lax.axis_size(axis)
    pairs = [(source, (source + steps) % count) for source in range(count)]
    return lax.ppermute(value, axis, pairs)


def attend_block(joined_ref, head, start, stop):
    scale = 1.0 / (HDIM**0.5)

    def part(which):
        return pl.ds(pl.multiple_of((3 * head + which) * HDIM, HDIM), HDIM)

    query = joined_ref[start:stop, part(0)]
    keys = joined_ref[:stop, part(1)]
    vals = joined_ref[:stop, part(2)]
    scores = (
        lax.dot_general(query, keys, (((1,), (1,)), ((), ())), preferred_element_type=jnp.float32)
        * scale
    )
    rows = start + lax.broadcasted_iota(jnp.int32, scores.shape, 0)
    cols = lax.broadcasted_iota(jnp.int32, scores.shape, 1)
    scores = jnp.where(cols <= rows, scores, jnp.float32(-1e30))
    top = jnp.max(scores, axis=1, keepdims=True)
    expd = jnp.exp(scores - top)
    probs = (expd * (1.0 / jnp.sum(expd, axis=1, keepdims=True))).astype(jnp.bfloat16)
    return jnp.dot(probs, vals, preferred_element_type=jnp.float32).astype(jnp.bfloat16)


def attend_heads(joined_ref, out_hbm, attended, sems):
    narrow_at = lax.axis_index("narrow")
    seq_len = joined_ref.shape[0]
    heads = attended.shape[0]
    count = seq_len // 2
    block = min(QBLOCK, count)
    partner = {"narrow": 1 - narrow_at}
    barrier = pltpu.get_barrier_semaphore()
    pl.semaphore_signal(barrier, inc=1, device_id=partner, device_id_type=MESH)
    pl.semaphore_wait(barrier, 1)

    def into(head):
        column = pl.multiple_of((narrow_at * heads + head) * HDIM, HDIM)
        return out_hbm.at[:, pl.ds(column, HDIM)]

    def send(head):
        return pltpu.make_async_remote_copy(
            src_ref=attended.at[head, 1 - narrow_at],
            dst_ref=into(head),
            send_sem=sems.at[0, head],
            recv_sem=sems.at[1, head],
            device_id=partner,
            device_id_type=MESH,
        )

    def keep(head):
        return pltpu.make_async_copy(attended.at[head, narrow_at], into(head), sems.at[2, head])

    def one(head, carry):
        for start in range(0, seq_len, block):
            at = start % count
            attended[head, start // count, at : at + block] = attend_block(
                joined_ref, head, start, start + block
            )
        send(head).start()
        keep(head).start()
        return carry

    lax.fori_loop(0, heads, one, 0)

    def finish(head, carry):
        send(head).wait()
        keep(head).wait()
        return carry

    lax.fori_loop(0, heads, finish, 0)


def attention(joined):
    seq_len, width = joined.shape
    heads = width // (3 * HDIM)
    count = seq_len // 2
    return pl.pallas_call(
        attend_heads,
        in_specs=[pl.BlockSpec(memory_space=pltpu.VMEM)],
        out_specs=pl.BlockSpec(memory_space=pl.ANY),
        out_shape=jax.ShapeDtypeStruct((count, 2 * heads * HDIM), jnp.bfloat16),
        scratch_shapes=[
            pltpu.VMEM((heads, 2, count, HDIM), jnp.bfloat16),
            pltpu.SemaphoreType.DMA((3, heads)),
        ],
        compiler_params=pltpu.CompilerParams(
            collective_id=2, has_side_effects=True, vmem_limit_bytes=40 << 20
        ),
        cost_estimate=pl.CostEstimate(
            flops=3 * heads * seq_len * seq_len * HDIM,
            bytes_accessed=4 * 2 * seq_len * heads * HDIM,
            transcendentals=heads * seq_len * seq_len // 2,
        ),
    )(joined)


def barrier_with(place, core, others):
    barrier = pltpu.get_barrier_semaphore()
    pl.semaphore_signal(barrier, inc=1, device_id={"wide": place * 2 + 1 - core}, device_id_type=MESH)
    for other in others:
        pl.semaphore_signal(barrier, inc=1, device_id=other, device_id_type=MESH)

    @pl.when(place > 0)
    def _():
        pl.semaphore_signal(
            barrier, inc=1, device_id={"wide": (place - 1) * 2 + core}, device_id_type=MESH
        )

    @pl.when(place < PLACES - 1)
    def _():
        pl.semaphore_signal(
            barrier, inc=1, device_id={"wide": (place + 1) * 2 + core}, device_id_type=MESH
        )

    count = 2 + len(others)

    @pl.when((place == 0) | (place == PLACES - 1))
    def _():
        pl.semaphore_wait(barrier, count)

    @pl.when((place > 0) & (place < PLACES - 1))
    def _():
        pl.semaphore_wait(barrier, count + 1)


def ffn_ends(
    steps, hidden_ref, weight_ref, resid_hbm, own_ref, raw_hbm, marks_ref,
    sums, swapped, line, resid, stream, raw, acc, parts,
    swap_sems, line_sems, cross_sems, raw_sems, resid_sem, part_sems,
):
    wide_at = lax.axis_index("wide")
    section_at = lax.axis_index("section")
    narrow_at = lax.axis_index("narrow")
    place, core = wide_at // 2, wide_at % 2
    step = pl.program_id(0)
    rows, cols = sums.shape[4], sums.shape[5]
    last = PLACES - 1
    at_end = (place == 0) | (place == last)
    across = {"section": 1 - section_at}
    beside = {"narrow": 1 - narrow_at}

    def fetch(kept):
        return pltpu.make_async_copy(resid_hbm.at[:, core, kept], resid, resid_sem)

    @pl.when(step == 0)
    def _():
        @pl.when(place == 0)
        def _():
            fetch(1).start()

        @pl.when(place == last)
        def _():
            fetch(0).start()

        barrier_with(place, core, (across, beside))
        acc[...] = jnp.zeros_like(acc)

    def swap(way, i):
        return pltpu.make_async_remote_copy(
            src_ref=sums.at[i, 1 - core, way],
            dst_ref=swapped.at[i, way],
            send_sem=swap_sems.at[way, 0, i],
            recv_sem=swap_sems.at[way, 1, i],
            device_id={"wide": place * 2 + 1 - core},
            device_id_type=MESH,
        )

    def pass_on(way, i):
        towards = place + 1 if way == 0 else place - 1
        return pltpu.make_async_remote_copy(
            src_ref=line.at[way, i],
            dst_ref=line.at[way, i],
            send_sem=line_sems.at[way, 0, i],
            recv_sem=line_sems.at[way, 1, i],
            device_id={"wide": towards * 2 + core},
            device_id_type=MESH,
        )

    def columns(i):
        return pl.ds(pl.multiple_of(i * cols, cols), cols)

    def cross(i):
        return pltpu.make_async_remote_copy(
            src_ref=stream.at[:, :, columns(i)],
            dst_ref=raw.at[:, :, columns(i)],
            send_sem=cross_sems.at[0, i],
            recv_sem=cross_sems.at[1, i],
            device_id=across,
            device_id_type=MESH,
        )

    def store(i):
        return pltpu.make_async_copy(
            raw.at[:, :, columns(i)], raw_hbm.at[:, :, columns(i)], raw_sems.at[i]
        )

    @pl.when(step < steps)
    def _():
        def tile(at, carry):
            start = pl.multiple_of(at * 4 * rows, 4 * rows)
            result = lax.dot_general(
                hidden_ref[pl.ds(start, 4 * rows), :],
                weight_ref[...],
                (((1,), (1,)), ((), ())),
                preferred_element_type=jnp.float32,
            )
            sums[step, :, :, at] = result.astype(jnp.bfloat16).reshape(2, 2, rows, cols)
            return carry

        lax.fori_loop(0, PLACES, tile, 0)
        for way in range(2):
            swap(way, step).start()

    for way in range(2):
        hops = place if way == 0 else last - place
        i = step - 1 - LAG * hops
        live = (i >= 0) & (i < steps)

        def mine(j):
            return sums[i, core, way, j].astype(jnp.float32) + swapped[i, way, j].astype(jnp.float32)

        @pl.when(live)
        def _():
            swap(way, i).wait_recv()

        @pl.when(live & (hops > 0))
        def _():
            pass_on(way, i).wait_recv()

        @pl.when(live & (hops == 0))
        def _():
            for j in range(PLACES):
                line[way, i, j] = mine(j).astype(jnp.bfloat16)

        @pl.when(live & (hops > 0) & (hops < last))
        def _():
            for j in range(PLACES):
                line[way, i, j] = (mine(j) + line[way, i, j].astype(jnp.float32)).astype(jnp.bfloat16)

        @pl.when(live & (hops < last))
        def _():
            pass_on(way, i).start()

        @pl.when(live & (hops == last))
        def _():
            @pl.when(i == 0)
            def _():
                fetch(way).wait()

            for j in range(PLACES):
                total = mine(j) + line[way, i, j].astype(jnp.float32)
                stream[j, :, columns(i)] = (
                    resid[j, :, columns(i)].astype(jnp.float32) + total
                ).astype(jnp.bfloat16)
            cross(i).start()

    came = step - 1 - LAG * last - CROSS_LAG

    @pl.when(at_end & (came >= 0) & (came < steps))
    def _():
        cross(came).wait_recv()
        store(came).start()
        for j in range(PLACES):
            values = raw[j, :, columns(came)].astype(jnp.float32)
            total, square = values[:, :LANES], values[:, :LANES] * values[:, :LANES]
            for at in range(LANES, cols, LANES):
                piece = values[:, at : at + LANES]
                total, square = total + piece, square + piece * piece
            acc[0, j] += total
            acc[1, j] += square

    @pl.when(step == steps + LAG * last + CROSS_LAG)
    def _():
        @pl.when(at_end)
        def _():
            lane = lax.broadcasted_iota(jnp.int32, (rows, LANES), 1)
            packed = jnp.zeros((rows, LANES), jnp.float32)
            for j in range(PLACES):
                for which in range(2):
                    total = jnp.sum(acc[which, j], axis=1, keepdims=True)
                    packed = jnp.where(lane == 2 * j + which, total, packed)
            parts[0] = packed
            exchange = pltpu.make_async_remote_copy(
                src_ref=parts.at[0],
                dst_ref=parts.at[1],
                send_sem=part_sems.at[0],
                recv_sem=part_sems.at[1],
                device_id=beside,
                device_id_type=MESH,
            )
            exchange.start()
            own_ref[...] = stream[place]
            exchange.wait()
            full = (parts[0] + parts[1]) / D
            marks = jnp.zeros((rows, LANES), jnp.float32)
            for j in range(PLACES):
                mean = full[:, 2 * j : 2 * j + 1]
                var = full[:, 2 * j + 1 : 2 * j + 2] - mean * mean
                marks = jnp.where(lane == 2 * j, mean, marks)
                marks = jnp.where(lane == 2 * j + 1, lax.rsqrt(var + 1e-05), marks)
            marks_ref[...] = marks

        def finish(i, carry):
            for way in range(2):
                hops = place if way == 0 else last - place
                swap(way, i).wait_send()

                @pl.when(hops < last)
                def _():
                    pass_on(way, i).wait_send()

            @pl.when(at_end)
            def _():
                cross(i).wait_send()
                store(i).wait()

            return carry

        lax.fori_loop(0, steps, finish, 0)


def ffn_rows(inner, down_weight, residual):
    seq_len, units = inner.shape
    width = down_weight.shape[0]
    cols = width // FFN_STEPS
    rows = seq_len // (4 * PLACES)
    last_step = FFN_STEPS - 1
    return pl.pallas_call(
        functools.partial(ffn_ends, FFN_STEPS),
        grid=(FFN_STEPS + LAG * (PLACES - 1) + CROSS_LAG + 1,),
        in_specs=[
            pl.BlockSpec((seq_len, units), lambda s: (0, 0), pipeline_mode=pl.Buffered(1)),
            pl.BlockSpec((cols, units), lambda s: (jnp.minimum(s, last_step), 0)),
            pl.BlockSpec(memory_space=pl.ANY),
        ],
        out_specs=[
            pl.BlockSpec((rows, width), lambda s: (0, 0), pipeline_mode=pl.Buffered(1)),
            pl.BlockSpec(memory_space=pl.ANY),
            pl.BlockSpec((rows, LANES), lambda s: (0, 0), pipeline_mode=pl.Buffered(1)),
        ],
        out_shape=[
            jax.ShapeDtypeStruct((rows, width), jnp.bfloat16),
            jax.ShapeDtypeStruct((PLACES, rows, width), jnp.bfloat16),
            jax.ShapeDtypeStruct((rows, LANES), jnp.float32),
        ],
        scratch_shapes=[
            pltpu.VMEM((FFN_STEPS, 2, 2, PLACES, rows, cols), jnp.bfloat16),
            pltpu.VMEM((FFN_STEPS, 2, PLACES, rows, cols), jnp.bfloat16),
            pltpu.VMEM((2, FFN_STEPS, PLACES, rows, cols), jnp.bfloat16),
            pltpu.VMEM((PLACES, rows, width), jnp.bfloat16),
            pltpu.VMEM((PLACES, rows, width), jnp.bfloat16),
            pltpu.VMEM((PLACES, rows, width), jnp.bfloat16),
            pltpu.VMEM((2, PLACES, rows, LANES), jnp.float32),
            pltpu.VMEM((2, rows, LANES), jnp.float32),
            pltpu.SemaphoreType.DMA((2, 2, FFN_STEPS)),
            pltpu.SemaphoreType.DMA((2, 2, FFN_STEPS)),
            pltpu.SemaphoreType.DMA((2, FFN_STEPS)),
            pltpu.SemaphoreType.DMA((FFN_STEPS,)),
            pltpu.SemaphoreType.DMA,
            pltpu.SemaphoreType.DMA((2,)),
        ],
        compiler_params=pltpu.CompilerParams(
            collective_id=0, has_side_effects=True, vmem_limit_bytes=60 << 20
        ),
        cost_estimate=pl.CostEstimate(
            flops=2 * seq_len * units * width, bytes_accessed=2 * units * width, transcendentals=0
        ),
    )(inner, down_weight, residual.reshape(PLACES, 2, 2, rows, width))


def qkv_gather(
    raw_hbm, marks_in, own_hbm, gain_ref, bias_ref, weight_hbm, out_ref, mine_hbm,
    line, marks, rows_of, weight, sending, coming,
    weight_sem, raw_sem, own_sem, mark_sems, line_sems, share_sems, back_sems, swap_sems, free_sem,
):
    wide_at = lax.axis_index("wide")
    section_at = lax.axis_index("section")
    narrow_at = lax.axis_index("narrow")
    place, core = wide_at // 2, wide_at % 2
    last = PLACES - 1
    tiles, tile_rows, tile_cols = sending.shape[1:]
    half = tiles * tile_cols
    rows, depth = rows_of.shape[3:]
    cols = depth // PIECES
    pieces = PLACES * PIECES
    across = {"section": 1 - section_at}
    partner = {"narrow": 1 - narrow_at}
    twin = {"wide": place * 2 + 1 - core}

    fetch = pltpu.make_async_copy(weight_hbm, weight, weight_sem)

    def begin(kept):
        return pltpu.make_async_copy(raw_hbm, line.at[kept], raw_sem)

    def settle(kept):
        return pltpu.make_async_copy(own_hbm, mine_hbm.at[pl.ds(kept * rows, rows)], own_sem)

    def at_source(kept):
        return place == (last if kept == 0 else 0)

    for kept in range(2):

        @pl.when(at_source(kept))
        def _():
            begin(kept).start()
            settle(kept).start()
            marks[kept] = marks_in[...]

    fetch.start()
    barrier_with(place, core, (across, partner))
    for kept in range(2):

        @pl.when(at_source(kept))
        def _():
            begin(kept).wait()

    def onwards(way):
        return {"wide": (place - 1 if way == 0 else place + 1) * 2 + core}

    def columns(q):
        return pl.ds(pl.multiple_of(q * cols, cols), cols)

    def pass_marks(way):
        return pltpu.make_async_remote_copy(
            src_ref=marks.at[way],
            dst_ref=marks.at[way],
            send_sem=mark_sems.at[way, 0],
            recv_sem=mark_sems.at[way, 1],
            device_id=onwards(way),
            device_id_type=MESH,
        )

    def pass_on(way, i):
        part = line.at[way, i // PIECES, :, columns(i % PIECES)]
        return pltpu.make_async_remote_copy(
            src_ref=part,
            dst_ref=part,
            send_sem=line_sems.at[way, 0, i],
            recv_sem=line_sems.at[way, 1, i],
            device_id=onwards(way),
            device_id_type=MESH,
        )

    def give_back(way, q):
        return pltpu.make_async_remote_copy(
            src_ref=line.at[way, place, :, columns(q)],
            dst_ref=mine_hbm.at[pl.ds(way * rows, rows), columns(q)],
            send_sem=back_sems.at[way, 0, q],
            recv_sem=back_sems.at[way, 1, q],
            device_id=across,
            device_id_type=MESH,
        )

    def share(way, i):
        part = rows_of.at[(i // PIECES) % 2, core, way, :, columns(i % PIECES)]
        return pltpu.make_async_remote_copy(
            src_ref=part,
            dst_ref=part,
            send_sem=share_sems.at[way, 0, i],
            recv_sem=share_sems.at[way, 1, i],
            device_id=twin,
            device_id_type=MESH,
        )

    def swap(phase, tile):
        return pltpu.make_async_remote_copy(
            src_ref=sending.at[phase, tile],
            dst_ref=coming.at[phase, tile],
            send_sem=swap_sems.at[0, phase, tile],
            recv_sem=swap_sems.at[1, phase, tile],
            device_id=partner,
            device_id_type=MESH,
        )

    def hops_of(way):
        return last - place if way == 0 else place

    def multiply(slot, column):
        return lax.dot_general(
            rows_of[slot].reshape(tile_rows, depth),
            weight[:, pl.ds(pl.multiple_of(column, tile_cols), tile_cols)],
            (((1,), (0,)), ((), ())),
            preferred_element_type=jnp.float32,
        )

    def take(phase, tile):
        swap(phase, tile).wait_recv()
        at = pl.ds(pl.multiple_of(tile * tile_cols, tile_cols), tile_cols)
        both = out_ref[phase, :, at].astype(jnp.float32) + coming[phase, tile].astype(jnp.float32)
        out_ref[phase, :, at] = both.astype(jnp.bfloat16)

    def tick(n, carry):
        for way in range(2):
            hops = hops_of(way)
            i = n - LAG * hops
            live = (i >= 0) & (i < pieces)

            @pl.when(live & (hops > 0) & (i == 0))
            def _():
                pass_marks(way).wait_recv()

            @pl.when(live & (hops > 0))
            def _():
                pass_on(way, i).wait_recv()

            @pl.when(live & (hops < last) & (i == 0))
            def _():
                pass_marks(way).start()

            @pl.when(live & (hops < last))
            def _():
                pass_on(way, i).start()

            @pl.when(live & (hops > 0) & (i // PIECES == place))
            def _():
                give_back(way, i % PIECES).start()

        e = n - LAG * last

        @pl.when((e >= 0) & (e < pieces))
        def _():
            phase, q = e // PIECES, e % PIECES

            @pl.when((phase >= 2) & (q == 0))
            def _():
                pl.semaphore_wait(free_sem, 1)

            lane = lax.broadcasted_iota(jnp.int32, (rows, LANES), 1)
            at = columns(q)
            @pl.when(phase >= 2)
            def _():
                for way in range(2):
                    share(way, e - 2 * PIECES).wait_send()

            for way in range(2):
                both = marks[way]
                mean = jnp.sum(jnp.where(lane == 2 * phase, both, 0.0), axis=1, keepdims=True)
                rstd = jnp.sum(jnp.where(lane == 2 * phase + 1, both, 0.0), axis=1, keepdims=True)
                values = line[way, phase, :, at].astype(jnp.float32)
                rows_of[phase % 2, core, way, :, at] = (
                    (values - mean) * rstd * gain_ref[:, at] + bias_ref[:, at]
                ).astype(jnp.bfloat16)
                share(way, e).start()

        d = e - PIECES
        phase, tile = d // PIECES, d % PIECES

        @pl.when((d >= 0) & (d < pieces))
        def _():
            @pl.when(d == 0)
            def _():
                fetch.wait()

            @pl.when(tile == 0)
            def _():
                def arrived(q, carry):
                    for way in range(2):
                        share(way, phase * PIECES + q).wait_recv()
                    return carry

                lax.fori_loop(0, PIECES, arrived, 0)

            away = tile < tiles
            column = jnp.where(
                away,
                (1 - narrow_at) * half + tile * tile_cols,
                narrow_at * half + (tile - tiles) * tile_cols,
            )
            product = multiply(phase % 2, column).astype(jnp.bfloat16)

            @pl.when(away)
            def _():
                sending[phase, tile] = product
                swap(phase, tile).start()

            @pl.when(tile >= tiles)
            def _():
                kept = pl.ds(pl.multiple_of((tile - tiles) * tile_cols, tile_cols), tile_cols)
                out_ref[phase, :, kept] = product

            @pl.when((tile == PIECES - 1) & (phase < PLACES - 2))
            def _():
                pl.semaphore_signal(free_sem, inc=1, device_id=twin, device_id_type=MESH)

        t = d - tiles - TAKE_LAG
        taken, of = t // PIECES, t % PIECES

        @pl.when((t >= 0) & (t < pieces) & (of < tiles))
        def _():
            take(taken, of)

        return carry

    lax.fori_loop(0, LAG * last + PIECES + pieces + TAKE_LAG, tick, 0)

    def finish(i, carry):
        for way in range(2):

            @pl.when(i >= 2 * PIECES)
            def _():
                share(way, i).wait_send()

            @pl.when(hops_of(way) < last)
            def _():
                pass_on(way, i).wait_send()

        return carry

    lax.fori_loop(0, pieces, finish, 0)

    for way in range(2):

        @pl.when(hops_of(way) < last)
        def _():
            pass_marks(way).wait_send()

        @pl.when(hops_of(way) > 0)
        def _():
            for q in range(PIECES):
                give_back(way, q).wait()

        @pl.when(at_source(way))
        def _():
            settle(way).wait()

    for phase in range(PLACES):
        for tile in range(tiles):
            swap(phase, tile).wait_send()


def qkv_rows(raw, marks, own, gain, bias, qkv_weight):
    rows, depth = raw.shape[1:]
    width = qkv_weight.shape[1]
    half = width // 2
    tiles = PIECES // 2
    passed = (PLACES, tiles, 4 * rows, half // tiles)
    pieces = PLACES * PIECES
    vmem = pl.BlockSpec(memory_space=pltpu.VMEM)
    hbm = pl.BlockSpec(memory_space=pl.ANY)
    return pl.pallas_call(
        qkv_gather,
        in_specs=[hbm, vmem, hbm, vmem, vmem, hbm],
        out_specs=[vmem, hbm],
        out_shape=[
            jax.ShapeDtypeStruct((PLACES, 4 * rows, half), jnp.bfloat16),
            jax.ShapeDtypeStruct((2 * rows, depth), jnp.bfloat16),
        ],
        scratch_shapes=[
            pltpu.VMEM((2, PLACES, rows, depth), jnp.bfloat16),
            pltpu.VMEM((2, rows, LANES), jnp.float32),
            pltpu.VMEM((2, 2, 2, rows, depth), jnp.bfloat16),
            pltpu.VMEM((depth, width), jnp.bfloat16),
            pltpu.VMEM(passed, jnp.bfloat16),
            pltpu.VMEM(passed, jnp.bfloat16),
            pltpu.SemaphoreType.DMA,
            pltpu.SemaphoreType.DMA,
            pltpu.SemaphoreType.DMA,
            pltpu.SemaphoreType.DMA((2, 2)),
            pltpu.SemaphoreType.DMA((2, 2, pieces)),
            pltpu.SemaphoreType.DMA((2, 2, pieces)),
            pltpu.SemaphoreType.DMA((2, 2, PIECES)),
            pltpu.SemaphoreType.DMA((2, PLACES, tiles)),
            pltpu.SemaphoreType.REGULAR,
        ],
        compiler_params=pltpu.CompilerParams(
            collective_id=1, has_side_effects=True, vmem_limit_bytes=63 << 20
        ),
        cost_estimate=pl.CostEstimate(
            flops=2 * 4 * PLACES * rows * depth * width,
            bytes_accessed=2 * depth * width,
            transcendentals=0,
        ),
    )(raw, marks, own, gain, bias, qkv_weight)


def split_heads(hidden, down_weight, residual, ln_gain, ln_bias, qkv_weight):
    seq_len = hidden.shape[1]
    half = qkv_weight.shape[1] // 2
    own, raw, marks = ffn_rows(hidden[0], down_weight, residual[0])
    joined, mine = qkv_rows(raw, marks, own, ln_gain[None], ln_bias[None], qkv_weight)
    attended = attention(joined.reshape(seq_len, half))
    return (mine[None], attended[None])


def split_queries(hidden, down_weight, residual, ln_gain, ln_bias, qkv_weight):
    inner = hidden[0]
    resid = residual[0]
    seq_len = inner.shape[0]
    wide_rows = seq_len // lax.axis_size("wide")
    wide_at = lax.axis_index("wide")
    contract = (((1,), (1,)), ((), ()))
    partial_ffn = lax.dot_general(inner, down_weight, contract, preferred_element_type=jnp.float32)
    summed = lax.psum(partial_ffn, "wide")
    mine = (resid.astype(jnp.float32) + summed).astype(jnp.bfloat16)
    arrived = from_behind(mine, "section", 1)
    own_rows = lax.dynamic_slice_in_dim(mine, wide_at * wide_rows, wide_rows, 0)
    values = arrived.astype(jnp.float32)
    totals, squares = lax.psum(
        (jnp.sum(values, axis=1), jnp.sum(values * values, axis=1)), "narrow"
    )
    mean = totals / D
    var = squares / D - mean * mean
    normed = (
        (values - mean[:, None]) * lax.rsqrt(var + 1e-05)[:, None] * ln_gain + ln_bias
    ).astype(jnp.bfloat16)
    heads_here = qkv_weight.shape[1] // (3 * HDIM)
    query_count = seq_len // lax.axis_size("narrow")
    narrow_at = lax.axis_index("narrow")
    joined = lax.psum(
        jnp.dot(normed, qkv_weight, preferred_element_type=jnp.float32), "narrow"
    ).astype(jnp.bfloat16)
    mine_joined = lax.dynamic_slice_in_dim(joined, narrow_at * query_count, query_count, 0)
    query = mine_joined.reshape(query_count, heads_here, 3, HDIM)[:, :, 0]
    pairs = joined.reshape(seq_len, heads_here, 3, HDIM)[:, :, 1:]
    keys = pairs[:, :, 0]
    vals = pairs[:, :, 1]
    scores = jnp.einsum("qhd,khd->hqk", query, keys, preferred_element_type=jnp.float32) / jnp.sqrt(
        jnp.float32(HDIM)
    )
    query_pos = narrow_at * query_count + lax.broadcasted_iota(jnp.int32, (query_count, seq_len), 0)
    key_pos = lax.broadcasted_iota(jnp.int32, (query_count, seq_len), 1)
    scores = jnp.where((key_pos <= query_pos)[None], scores, jnp.float32(-1e30))
    top = jnp.max(scores, axis=2, keepdims=True)
    expd = jnp.exp(scores - top)
    probs = (expd / jnp.sum(expd, axis=2, keepdims=True)).astype(jnp.bfloat16)
    attended = jnp.einsum("hqk,khd->qhd", probs, vals, preferred_element_type=jnp.float32).astype(
        jnp.bfloat16
    )
    attended = attended.reshape(query_count, heads_here * HDIM)
    return (own_rows[None], attended[None])


def per_device(hidden, down_weight, residual, ln_gain, ln_bias, qkv_weight):
    heads_here = qkv_weight.shape[1] // (3 * HDIM)
    wide_rows = hidden.shape[1] // lax.axis_size("wide")
    even = heads_here % 8 == 0 and wide_rows % 32 == 0
    line = lax.axis_size("section") == 2 and lax.axis_size("wide") == 2 * PLACES and lax.axis_size("narrow") == 2
    even = even and down_weight.shape[0] % (FFN_STEPS * 128) == 0
    plan = split_heads if line and even else split_queries
    return plan(hidden, down_weight, residual, ln_gain, ln_bias, qkv_weight)


def solution(mesh):
    return jax.shard_map(
        per_device,
        mesh=mesh,
        in_specs=(
            P("section", None, "wide"),
            P("narrow", "wide"),
            P("section", None, "narrow"),
            P("narrow"),
            P("narrow"),
            P("narrow", "wide"),
        ),
        out_specs=(P("section", "wide", "narrow"), P("section", "narrow", "wide")),
        check_vma=False,
    )
```

```python
import functools

import jax
import jax.numpy as jnp
from jax import lax
from jax.experimental import pallas as pl
from jax.experimental.pallas import tpu as pltpu
from jax.sharding import PartitionSpec as P

D = 12288
HDIM = 128
LANES = 128
PLACES = 4
FFN_STEPS = 24
PIECES = 6
LAG = 2
CROSS_LAG = 2
TAKE_LAG = 3
MESH = pl.DeviceIdType.MESH


def from_behind(value, axis, steps):
    count = lax.axis_size(axis)
    pairs = [(source, (source + steps) % count) for source in range(count)]
    return lax.ppermute(value, axis, pairs)


def attend_block(joined_ref, head, block):
    factor = 1.4426950408889634 / (HDIM**0.5)
    size = joined_ref.shape[1]

    def part(which):
        return pl.ds(pl.multiple_of((3 * head + which) * HDIM, HDIM), HDIM)

    def scores_of(keys):
        return lax.dot_general(query, keys, (((1,), (1,)), ((), ())), preferred_element_type=jnp.float32)

    query = joined_ref[block, :, part(0)]
    shape = (size, size)
    seen = lax.broadcasted_iota(jnp.int32, shape, 1) <= lax.broadcasted_iota(jnp.int32, shape, 0)
    near = jnp.where(seen, scores_of(joined_ref[block, :, part(1)]), jnp.float32(-1e30))
    top = jnp.max(near, axis=1, keepdims=True)
    if block:
        far = scores_of(joined_ref[:block, :, part(1)].reshape(block * size, HDIM))
        top = jnp.maximum(top, jnp.max(far, axis=1, keepdims=True))
    near = jnp.exp2((near - top) * factor)
    total = jnp.sum(near, axis=1, keepdims=True)
    out = jnp.dot(
        near.astype(jnp.bfloat16), joined_ref[block, :, part(2)], preferred_element_type=jnp.float32
    )
    if block:
        far = jnp.exp2((far - top) * factor)
        total += jnp.sum(far, axis=1, keepdims=True)
        out += jnp.dot(
            far.astype(jnp.bfloat16),
            joined_ref[:block, :, part(2)].reshape(block * size, HDIM),
            preferred_element_type=jnp.float32,
        )
    return (out * (1.0 / total)).astype(jnp.bfloat16)


def barrier_with(place, core, others):
    barrier = pltpu.get_barrier_semaphore()
    pl.semaphore_signal(barrier, inc=1, device_id={"wide": place * 2 + 1 - core}, device_id_type=MESH)
    for other in others:
        pl.semaphore_signal(barrier, inc=1, device_id=other, device_id_type=MESH)

    @pl.when(place > 0)
    def _():
        pl.semaphore_signal(
            barrier, inc=1, device_id={"wide": (place - 1) * 2 + core}, device_id_type=MESH
        )

    @pl.when(place < PLACES - 1)
    def _():
        pl.semaphore_signal(
            barrier, inc=1, device_id={"wide": (place + 1) * 2 + core}, device_id_type=MESH
        )

    count = 2 + len(others)

    @pl.when((place == 0) | (place == PLACES - 1))
    def _():
        pl.semaphore_wait(barrier, count)

    @pl.when((place > 0) & (place < PLACES - 1))
    def _():
        pl.semaphore_wait(barrier, count + 1)


def ffn_ends(
    steps, hidden_ref, weight_ref, resid_hbm, own_ref, raw_hbm, marks_ref,
    sums, swapped, line, resid, stream, raw, acc, parts,
    swap_sems, line_sems, cross_sems, raw_sems, resid_sem, part_sems,
):
    wide_at = lax.axis_index("wide")
    section_at = lax.axis_index("section")
    narrow_at = lax.axis_index("narrow")
    place, core = wide_at // 2, wide_at % 2
    step = pl.program_id(0)
    rows, cols = sums.shape[4], sums.shape[5]
    last = PLACES - 1
    at_end = (place == 0) | (place == last)
    across = {"section": 1 - section_at}
    beside = {"narrow": 1 - narrow_at}

    def fetch(kept):
        return pltpu.make_async_copy(resid_hbm.at[:, core, kept], resid, resid_sem)

    @pl.when(step == 0)
    def _():
        @pl.when(place == 0)
        def _():
            fetch(1).start()

        @pl.when(place == last)
        def _():
            fetch(0).start()

        barrier_with(place, core, (across, beside))
        acc[...] = jnp.zeros_like(acc)

    def swap(way, i):
        return pltpu.make_async_remote_copy(
            src_ref=sums.at[i, 1 - core, way],
            dst_ref=swapped.at[i, way],
            send_sem=swap_sems.at[way, 0, i],
            recv_sem=swap_sems.at[way, 1, i],
            device_id={"wide": place * 2 + 1 - core},
            device_id_type=MESH,
        )

    def pass_on(way, i):
        towards = place + 1 if way == 0 else place - 1
        return pltpu.make_async_remote_copy(
            src_ref=line.at[way, i],
            dst_ref=line.at[way, i],
            send_sem=line_sems.at[way, 0, i],
            recv_sem=line_sems.at[way, 1, i],
            device_id={"wide": towards * 2 + core},
            device_id_type=MESH,
        )

    def columns(i):
        return pl.ds(pl.multiple_of(i * cols, cols), cols)

    def cross(i):
        return pltpu.make_async_remote_copy(
            src_ref=stream.at[:, :, columns(i)],
            dst_ref=raw.at[:, :, columns(i)],
            send_sem=cross_sems.at[0, i],
            recv_sem=cross_sems.at[1, i],
            device_id=across,
            device_id_type=MESH,
        )

    def store(i):
        return pltpu.make_async_copy(
            raw.at[:, :, columns(i)], raw_hbm.at[:, :, columns(i)], raw_sems.at[i]
        )

    @pl.when(step < steps)
    def _():
        result = lax.dot_general(
            hidden_ref[...], weight_ref[...], (((1,), (1,)), ((), ())), preferred_element_type=jnp.float32
        ).astype(jnp.bfloat16)
        for j in range(PLACES):
            part = result[4 * rows * j : 4 * rows * (j + 1)]
            sums[step, :, :, j] = part.reshape(2, 2, rows, cols)
        for way in range(2):
            swap(way, step).start()

    for way in range(2):
        hops = place if way == 0 else last - place
        i = step - 1 - LAG * hops
        live = (i >= 0) & (i < steps)

        def mine(j):
            return sums[i, core, way, j].astype(jnp.float32) + swapped[i, way, j].astype(jnp.float32)

        @pl.when(live)
        def _():
            swap(way, i).wait_recv()

        @pl.when(live & (hops > 0))
        def _():
            pass_on(way, i).wait_recv()

        @pl.when(live & (hops == 0))
        def _():
            for j in range(PLACES):
                line[way, i, j] = mine(j).astype(jnp.bfloat16)

        @pl.when(live & (hops > 0) & (hops < last))
        def _():
            for j in range(PLACES):
                line[way, i, j] = (mine(j) + line[way, i, j].astype(jnp.float32)).astype(jnp.bfloat16)

        @pl.when(live & (hops < last))
        def _():
            pass_on(way, i).start()

        @pl.when(live & (hops == last))
        def _():
            @pl.when(i == 0)
            def _():
                fetch(way).wait()

            for j in range(PLACES):
                total = mine(j) + line[way, i, j].astype(jnp.float32)
                stream[j, :, columns(i)] = (
                    resid[j, :, columns(i)].astype(jnp.float32) + total
                ).astype(jnp.bfloat16)
            cross(i).start()

    came = step - 1 - LAG * last - CROSS_LAG

    @pl.when(at_end & (came >= 0) & (came < steps))
    def _():
        cross(came).wait_recv()
        store(came).start()
        for j in range(PLACES):
            values = raw[j, :, columns(came)].astype(jnp.float32)
            total, square = values[:, :LANES], values[:, :LANES] * values[:, :LANES]
            for at in range(LANES, cols, LANES):
                piece = values[:, at : at + LANES]
                total, square = total + piece, square + piece * piece
            acc[0, j] += total
            acc[1, j] += square

    @pl.when(step == steps + LAG * last + CROSS_LAG)
    def _():
        @pl.when(at_end)
        def _():
            lane = lax.broadcasted_iota(jnp.int32, (rows, LANES), 1)
            packed = jnp.zeros((rows, LANES), jnp.float32)
            for j in range(PLACES):
                for which in range(2):
                    total = jnp.sum(acc[which, j], axis=1, keepdims=True)
                    packed = jnp.where(lane == 2 * j + which, total, packed)
            parts[0] = packed
            exchange = pltpu.make_async_remote_copy(
                src_ref=parts.at[0],
                dst_ref=parts.at[1],
                send_sem=part_sems.at[0],
                recv_sem=part_sems.at[1],
                device_id=beside,
                device_id_type=MESH,
            )
            exchange.start()
            own_ref[...] = stream[place]
            exchange.wait()
            full = (parts[0] + parts[1]) / D
            marks = jnp.zeros((rows, LANES), jnp.float32)
            for j in range(PLACES):
                mean = full[:, 2 * j : 2 * j + 1]
                var = full[:, 2 * j + 1 : 2 * j + 2] - mean * mean
                marks = jnp.where(lane == 2 * j, mean, marks)
                marks = jnp.where(lane == 2 * j + 1, lax.rsqrt(var + 1e-05), marks)
            marks_ref[...] = marks

        def finish(i, carry):
            for way in range(2):
                hops = place if way == 0 else last - place
                swap(way, i).wait_send()

                @pl.when(hops < last)
                def _():
                    pass_on(way, i).wait_send()

            @pl.when(at_end)
            def _():
                cross(i).wait_send()
                store(i).wait()

            return carry

        lax.fori_loop(0, steps, finish, 0)


def ffn_rows(inner, down_weight, residual):
    seq_len, units = inner.shape
    width = down_weight.shape[0]
    cols = width // FFN_STEPS
    rows = seq_len // (4 * PLACES)
    last_step = FFN_STEPS - 1
    return pl.pallas_call(
        functools.partial(ffn_ends, FFN_STEPS),
        grid=(FFN_STEPS + LAG * (PLACES - 1) + CROSS_LAG + 1,),
        in_specs=[
            pl.BlockSpec((seq_len, units), lambda s: (0, 0), pipeline_mode=pl.Buffered(1)),
            pl.BlockSpec((cols, units), lambda s: (jnp.minimum(s, last_step), 0)),
            pl.BlockSpec(memory_space=pl.ANY),
        ],
        out_specs=[
            pl.BlockSpec((rows, width), lambda s: (0, 0), pipeline_mode=pl.Buffered(1)),
            pl.BlockSpec(memory_space=pl.ANY),
            pl.BlockSpec((rows, LANES), lambda s: (0, 0), pipeline_mode=pl.Buffered(1)),
        ],
        out_shape=[
            jax.ShapeDtypeStruct((rows, width), jnp.bfloat16),
            jax.ShapeDtypeStruct((PLACES, rows, width), jnp.bfloat16),
            jax.ShapeDtypeStruct((rows, LANES), jnp.float32),
        ],
        scratch_shapes=[
            pltpu.VMEM((FFN_STEPS, 2, 2, PLACES, rows, cols), jnp.bfloat16),
            pltpu.VMEM((FFN_STEPS, 2, PLACES, rows, cols), jnp.bfloat16),
            pltpu.VMEM((2, FFN_STEPS, PLACES, rows, cols), jnp.bfloat16),
            pltpu.VMEM((PLACES, rows, width), jnp.bfloat16),
            pltpu.VMEM((PLACES, rows, width), jnp.bfloat16),
            pltpu.VMEM((PLACES, rows, width), jnp.bfloat16),
            pltpu.VMEM((2, PLACES, rows, LANES), jnp.float32),
            pltpu.VMEM((2, rows, LANES), jnp.float32),
            pltpu.SemaphoreType.DMA((2, 2, FFN_STEPS)),
            pltpu.SemaphoreType.DMA((2, 2, FFN_STEPS)),
            pltpu.SemaphoreType.DMA((2, FFN_STEPS)),
            pltpu.SemaphoreType.DMA((FFN_STEPS,)),
            pltpu.SemaphoreType.DMA,
            pltpu.SemaphoreType.DMA((2,)),
        ],
        compiler_params=pltpu.CompilerParams(
            collective_id=0, has_side_effects=True, vmem_limit_bytes=60 << 20
        ),
        cost_estimate=pl.CostEstimate(
            flops=2 * seq_len * units * width, bytes_accessed=2 * units * width, transcendentals=0
        ),
    )(inner, down_weight, residual.reshape(PLACES, 2, 2, rows, width))


def qkv_attend(
    raw_hbm, marks_in, own_hbm, gain_ref, bias_ref, weight_hbm, out_hbm, mine_hbm,
    line, marks, rows_of, weight, sending, coming, joined, attended,
    weight_sem, raw_sem, own_sem, mark_sems, line_sems, share_sems, back_sems, swap_sems, out_sems,
    free_sems,
):
    wide_at = lax.axis_index("wide")
    section_at = lax.axis_index("section")
    narrow_at = lax.axis_index("narrow")
    place, core = wide_at // 2, wide_at % 2
    last = PLACES - 1
    tiles, tile_rows, tile_cols = sending.shape[2:]
    half = tiles * tile_cols
    rows, depth = rows_of.shape[3:]
    cols = depth // PIECES
    pieces = PLACES * PIECES
    heads = attended.shape[1]
    across = {"section": 1 - section_at}
    partner = {"narrow": 1 - narrow_at}
    twin = {"wide": place * 2 + 1 - core}

    fetch = pltpu.make_async_copy(weight_hbm, weight, weight_sem)

    def begin(kept):
        return pltpu.make_async_copy(raw_hbm, line.at[kept], raw_sem)

    def settle(kept):
        return pltpu.make_async_copy(own_hbm, mine_hbm.at[pl.ds(kept * rows, rows)], own_sem)

    def at_source(kept):
        return place == (last if kept == 0 else 0)

    for kept in range(2):

        @pl.when(at_source(kept))
        def _():
            begin(kept).start()
            settle(kept).start()
            marks[kept] = marks_in[...]

    fetch.start()
    barrier_with(place, core, (across, partner))
    for kept in range(2):

        @pl.when(at_source(kept))
        def _():
            begin(kept).wait()

    def onwards(way):
        return {"wide": (place - 1 if way == 0 else place + 1) * 2 + core}

    def columns(q):
        return pl.ds(pl.multiple_of(q * cols, cols), cols)

    def pass_marks(way):
        return pltpu.make_async_remote_copy(
            src_ref=marks.at[way],
            dst_ref=marks.at[way],
            send_sem=mark_sems.at[way, 0],
            recv_sem=mark_sems.at[way, 1],
            device_id=onwards(way),
            device_id_type=MESH,
        )

    def pass_on(way, i):
        part = line.at[way, i // PIECES, :, columns(i % PIECES)]
        return pltpu.make_async_remote_copy(
            src_ref=part,
            dst_ref=part,
            send_sem=line_sems.at[way, 0, i],
            recv_sem=line_sems.at[way, 1, i],
            device_id=onwards(way),
            device_id_type=MESH,
        )

    def give_back(way, q):
        return pltpu.make_async_remote_copy(
            src_ref=line.at[way, place, :, columns(q)],
            dst_ref=mine_hbm.at[pl.ds(way * rows, rows), columns(q)],
            send_sem=back_sems.at[way, 0, q],
            recv_sem=back_sems.at[way, 1, q],
            device_id=across,
            device_id_type=MESH,
        )

    def share(way, i):
        part = rows_of.at[(i // PIECES) % 2, way, core, :, columns(i % PIECES)]
        return pltpu.make_async_remote_copy(
            src_ref=part,
            dst_ref=part,
            send_sem=share_sems.at[way, 0, i],
            recv_sem=share_sems.at[way, 1, i],
            device_id=twin,
            device_id_type=MESH,
        )

    def swap(way, phase, tile):
        return pltpu.make_async_remote_copy(
            src_ref=sending.at[way, phase, tile],
            dst_ref=coming.at[way, phase, tile],
            send_sem=swap_sems.at[way, 0, phase, tile],
            recv_sem=swap_sems.at[way, 1, phase, tile],
            device_id=partner,
            device_id_type=MESH,
        )

    def into(block, head):
        row = pl.ds((block % 2) * 4 * rows, 4 * rows)
        column = pl.ds(pl.multiple_of((narrow_at * heads + head) * HDIM, HDIM), HDIM)
        return out_hbm.at[row, column]

    def deliver(block, head):
        return pltpu.make_async_remote_copy(
            src_ref=attended.at[block, head],
            dst_ref=into(block, head),
            send_sem=out_sems.at[0, block % 2, head],
            recv_sem=out_sems.at[1, block % 2, head],
            device_id=partner,
            device_id_type=MESH,
        )

    def keep(block, head):
        return pltpu.make_async_copy(
            attended.at[block, head], into(block, head), out_sems.at[2, block % 2, head]
        )

    def hops_of(way):
        return last - place if way == 0 else place

    def tile_at(tile):
        return pl.ds(pl.multiple_of(tile * tile_cols, tile_cols), tile_cols)

    def arrive(way, n):
        hops = hops_of(way)
        i = n - LAG * hops
        phase, q = i // PIECES, i % PIECES

        @pl.when((i >= 0) & (i < pieces))
        def _():
            @pl.when(hops > 0)
            def _():
                @pl.when(i == 0)
                def _():
                    pass_marks(way).wait_recv()

                pass_on(way, i).wait_recv()

            @pl.when(hops < last)
            def _():
                @pl.when(i == 0)
                def _():
                    pass_marks(way).start()

                pass_on(way, i).start()

            @pl.when((hops > 0) & (phase == place))
            def _():
                give_back(way, q).start()

            @pl.when((phase >= 2) & (q == 0))
            def _():
                pl.semaphore_wait(free_sems.at[way], 1)

            @pl.when(phase >= 2)
            def _():
                share(way, i - 2 * PIECES).wait_send()

            lane = lax.broadcasted_iota(jnp.int32, (rows, LANES), 1)
            at = columns(q)
            both = marks[way]
            mean = jnp.sum(jnp.where(lane == 2 * phase, both, 0.0), axis=1, keepdims=True)
            rstd = jnp.sum(jnp.where(lane == 2 * phase + 1, both, 0.0), axis=1, keepdims=True)
            values = line[way, phase, :, at].astype(jnp.float32)
            rows_of[phase % 2, way, core, :, at] = (
                (values - mean) * rstd * gain_ref[:, at] + bias_ref[:, at]
            ).astype(jnp.bfloat16)
            share(way, i).start()

    def project(way, n):
        d = n - LAG * hops_of(way) - PIECES
        phase, tile = d // PIECES, d % PIECES

        @pl.when((d >= 0) & (d < pieces))
        def _():
            @pl.when(tile == 0)
            def _():
                def arrived(q, carry):
                    share(way, phase * PIECES + q).wait_recv()
                    return carry

                lax.fori_loop(0, PIECES, arrived, 0)

            away = tile < tiles
            column = jnp.where(
                away,
                (1 - narrow_at) * half + tile * tile_cols,
                narrow_at * half + (tile - tiles) * tile_cols,
            )
            product = lax.dot_general(
                rows_of[phase % 2, way].reshape(tile_rows, depth),
                weight[:, pl.ds(pl.multiple_of(column, tile_cols), tile_cols)],
                (((1,), (0,)), ((), ())),
                preferred_element_type=jnp.float32,
            ).astype(jnp.bfloat16)

            @pl.when(away)
            def _():
                sending[way, phase, tile] = product
                swap(way, phase, tile).start()

            @pl.when(tile >= tiles)
            def _():
                for which in range(2):
                    at = pl.ds((2 * which + way) * rows, rows)
                    joined[phase, at, tile_at(tile - tiles)] = product[which * rows : (which + 1) * rows]

            @pl.when((tile == PIECES - 1) & (phase < PLACES - 2))
            def _():
                pl.semaphore_signal(free_sems.at[way], inc=1, device_id=twin, device_id_type=MESH)

        t = d - tiles - TAKE_LAG
        taken, of = t // PIECES, t % PIECES

        @pl.when((t >= 0) & (t < pieces) & (of < tiles))
        def _():
            swap(way, taken, of).wait_recv()
            for which in range(2):
                at = pl.ds((2 * which + way) * rows, rows)
                came = coming[way, taken, of, which * rows : (which + 1) * rows].astype(jnp.float32)
                both = joined[taken, at, tile_at(of)].astype(jnp.float32) + came
                joined[taken, at, tile_at(of)] = both.astype(jnp.bfloat16)

    whole = LAG * jnp.maximum(place, last - place) + PIECES + 2 * tiles + TAKE_LAG

    def tick(n, carry):
        for way in range(2):
            arrive(way, n)

        @pl.when(n == PIECES)
        def _():
            fetch.wait()

        for way in range(2):
            project(way, n)

        a = n - whole
        head = a % PIECES
        for block in range(PLACES):

            @pl.when((a // PIECES == block) & (head < heads) & (a >= 0))
            def _():
                attended[block, head] = attend_block(joined, head, block)

                @pl.when(narrow_at == block // 2)
                def _():
                    keep(block, head).start()

                @pl.when(narrow_at != block // 2)
                def _():
                    deliver(block, head).start()

        return carry

    lax.fori_loop(0, LAG * last + PIECES + 2 * tiles + TAKE_LAG + (PLACES - 1) * PIECES + heads, tick, 0)

    def finish(i, carry):
        for way in range(2):

            @pl.when(i >= 2 * PIECES)
            def _():
                share(way, i).wait_send()

            @pl.when(hops_of(way) < last)
            def _():
                pass_on(way, i).wait_send()

        return carry

    lax.fori_loop(0, pieces, finish, 0)

    for way in range(2):

        @pl.when(hops_of(way) < last)
        def _():
            pass_marks(way).wait_send()

        @pl.when(hops_of(way) > 0)
        def _():
            for q in range(PIECES):
                give_back(way, q).wait()

        @pl.when(at_source(way))
        def _():
            settle(way).wait()

        for phase in range(PLACES):
            for tile in range(tiles):
                swap(way, phase, tile).wait_send()

    for block in range(2):
        for head in range(heads):
            deliver(block, head).wait()
            keep(block, head).wait()


def qkv_rows(raw, marks, own, gain, bias, qkv_weight):
    rows, depth = raw.shape[1:]
    width = qkv_weight.shape[1]
    half = width // 2
    tiles = PIECES // 2
    heads = half // (3 * HDIM)
    passed = (2, PLACES, tiles, 2 * rows, half // tiles)
    pieces = PLACES * PIECES
    seq_len = 4 * PLACES * rows
    vmem = pl.BlockSpec(memory_space=pltpu.VMEM)
    hbm = pl.BlockSpec(memory_space=pl.ANY)
    return pl.pallas_call(
        qkv_attend,
        in_specs=[hbm, vmem, hbm, vmem, vmem, hbm],
        out_specs=[hbm, hbm],
        out_shape=[
            jax.ShapeDtypeStruct((seq_len // 2, 2 * heads * HDIM), jnp.bfloat16),
            jax.ShapeDtypeStruct((2 * rows, depth), jnp.bfloat16),
        ],
        scratch_shapes=[
            pltpu.VMEM((2, PLACES, rows, depth), jnp.bfloat16),
            pltpu.VMEM((2, rows, LANES), jnp.float32),
            pltpu.VMEM((2, 2, 2, rows, depth), jnp.bfloat16),
            pltpu.VMEM((depth, width), jnp.bfloat16),
            pltpu.VMEM(passed, jnp.bfloat16),
            pltpu.VMEM(passed, jnp.bfloat16),
            pltpu.VMEM((PLACES, 4 * rows, half), jnp.bfloat16),
            pltpu.VMEM((PLACES, heads, 4 * rows, HDIM), jnp.bfloat16),
            pltpu.SemaphoreType.DMA,
            pltpu.SemaphoreType.DMA,
            pltpu.SemaphoreType.DMA,
            pltpu.SemaphoreType.DMA((2, 2)),
            pltpu.SemaphoreType.DMA((2, 2, pieces)),
            pltpu.SemaphoreType.DMA((2, 2, pieces)),
            pltpu.SemaphoreType.DMA((2, 2, PIECES)),
            pltpu.SemaphoreType.DMA((2, 2, PLACES, tiles)),
            pltpu.SemaphoreType.DMA((3, 2, heads)),
            pltpu.SemaphoreType.REGULAR((2,)),
        ],
        compiler_params=pltpu.CompilerParams(
            collective_id=1, has_side_effects=True, vmem_limit_bytes=63 << 20
        ),
        cost_estimate=pl.CostEstimate(
            flops=2 * seq_len * depth * width + 3 * heads * seq_len * seq_len * HDIM,
            bytes_accessed=2 * depth * width,
            transcendentals=heads * seq_len * seq_len // 2,
        ),
    )(raw, marks, own, gain, bias, qkv_weight)


def split_heads(hidden, down_weight, residual, ln_gain, ln_bias, qkv_weight):
    own, raw, marks = ffn_rows(hidden[0], down_weight, residual[0])
    attended, mine = qkv_rows(raw, marks, own, ln_gain[None], ln_bias[None], qkv_weight)
    return (mine[None], attended[None])


def split_queries(hidden, down_weight, residual, ln_gain, ln_bias, qkv_weight):
    inner = hidden[0]
    resid = residual[0]
    seq_len = inner.shape[0]
    wide_rows = seq_len // lax.axis_size("wide")
    wide_at = lax.axis_index("wide")
    contract = (((1,), (1,)), ((), ()))
    partial_ffn = lax.dot_general(inner, down_weight, contract, preferred_element_type=jnp.float32)
    summed = lax.psum(partial_ffn, "wide")
    mine = (resid.astype(jnp.float32) + summed).astype(jnp.bfloat16)
    arrived = from_behind(mine, "section", 1)
    own_rows = lax.dynamic_slice_in_dim(mine, wide_at * wide_rows, wide_rows, 0)
    values = arrived.astype(jnp.float32)
    totals, squares = lax.psum(
        (jnp.sum(values, axis=1), jnp.sum(values * values, axis=1)), "narrow"
    )
    mean = totals / D
    var = squares / D - mean * mean
    normed = (
        (values - mean[:, None]) * lax.rsqrt(var + 1e-05)[:, None] * ln_gain + ln_bias
    ).astype(jnp.bfloat16)
    heads_here = qkv_weight.shape[1] // (3 * HDIM)
    query_count = seq_len // lax.axis_size("narrow")
    narrow_at = lax.axis_index("narrow")
    joined = lax.psum(
        jnp.dot(normed, qkv_weight, preferred_element_type=jnp.float32), "narrow"
    ).astype(jnp.bfloat16)
    mine_joined = lax.dynamic_slice_in_dim(joined, narrow_at * query_count, query_count, 0)
    query = mine_joined.reshape(query_count, heads_here, 3, HDIM)[:, :, 0]
    pairs = joined.reshape(seq_len, heads_here, 3, HDIM)[:, :, 1:]
    keys = pairs[:, :, 0]
    vals = pairs[:, :, 1]
    scores = jnp.einsum("qhd,khd->hqk", query, keys, preferred_element_type=jnp.float32) / jnp.sqrt(
        jnp.float32(HDIM)
    )
    query_pos = narrow_at * query_count + lax.broadcasted_iota(jnp.int32, (query_count, seq_len), 0)
    key_pos = lax.broadcasted_iota(jnp.int32, (query_count, seq_len), 1)
    scores = jnp.where((key_pos <= query_pos)[None], scores, jnp.float32(-1e30))
    top = jnp.max(scores, axis=2, keepdims=True)
    expd = jnp.exp(scores - top)
    probs = (expd / jnp.sum(expd, axis=2, keepdims=True)).astype(jnp.bfloat16)
    attended = jnp.einsum("hqk,khd->qhd", probs, vals, preferred_element_type=jnp.float32).astype(
        jnp.bfloat16
    )
    attended = attended.reshape(query_count, heads_here * HDIM)
    return (own_rows[None], attended[None])


def per_device(hidden, down_weight, residual, ln_gain, ln_bias, qkv_weight):
    heads_here = qkv_weight.shape[1] // (3 * HDIM)
    wide_rows = hidden.shape[1] // lax.axis_size("wide")
    even = heads_here % 8 == 0 and wide_rows % 32 == 0
    line = lax.axis_size("section") == 2 and lax.axis_size("wide") == 2 * PLACES and lax.axis_size("narrow") == 2
    even = even and down_weight.shape[0] % (FFN_STEPS * 128) == 0
    plan = split_heads if line and even else split_queries
    return plan(hidden, down_weight, residual, ln_gain, ln_bias, qkv_weight)


def solution(mesh):
    return jax.shard_map(
        per_device,
        mesh=mesh,
        in_specs=(
            P("section", None, "wide"),
            P("narrow", "wide"),
            P("section", None, "narrow"),
            P("narrow"),
            P("narrow"),
            P("narrow", "wide"),
        ),
        out_specs=(P("section", "wide", "narrow"), P("section", "narrow", "wide")),
        check_vma=False,
    )
```

```python
import functools

import jax
import jax.numpy as jnp
from jax import lax
from jax.experimental import pallas as pl
from jax.experimental.pallas import tpu as pltpu
from jax.sharding import PartitionSpec as P

D = 12288
HDIM = 128
LANES = 128
PLACES = 4
FFN_STEPS = 24
PIECES = 6
LAG = 2
CROSS_LAG = 2
TAKE_LAG = 3
COPIES = 4
MESH = pl.DeviceIdType.MESH


def from_behind(value, axis, steps):
    count = lax.axis_size(axis)
    pairs = [(source, (source + steps) % count) for source in range(count)]
    return lax.ppermute(value, axis, pairs)


def attend_block(joined_ref, head, block):
    factor = 1.4426950408889634 / (HDIM**0.5)
    size = joined_ref.shape[1]

    def part(which):
        return pl.ds(pl.multiple_of((3 * head + which) * HDIM, HDIM), HDIM)

    def scores_of(keys):
        return lax.dot_general(query, keys, (((1,), (1,)), ((), ())), preferred_element_type=jnp.float32)

    query = joined_ref[block, :, part(0)]
    shape = (size, size)
    seen = lax.broadcasted_iota(jnp.int32, shape, 1) <= lax.broadcasted_iota(jnp.int32, shape, 0)
    near = jnp.where(seen, scores_of(joined_ref[block, :, part(1)]), jnp.float32(-1e30))
    top = jnp.max(near, axis=1, keepdims=True)
    if block:
        far = scores_of(joined_ref[:block, :, part(1)].reshape(block * size, HDIM))
        top = jnp.maximum(top, jnp.max(far, axis=1, keepdims=True))
    near = jnp.exp2((near - top) * factor)
    total = jnp.sum(near, axis=1, keepdims=True)
    out = jnp.dot(
        near.astype(jnp.bfloat16), joined_ref[block, :, part(2)], preferred_element_type=jnp.float32
    )
    if block:
        far = jnp.exp2((far - top) * factor)
        total += jnp.sum(far, axis=1, keepdims=True)
        out += jnp.dot(
            far.astype(jnp.bfloat16),
            joined_ref[:block, :, part(2)].reshape(block * size, HDIM),
            preferred_element_type=jnp.float32,
        )
    return (out * (1.0 / total)).astype(jnp.bfloat16)


def greet(place, core, others):
    barrier = pltpu.get_barrier_semaphore()
    pl.semaphore_signal(barrier, inc=1, device_id={"wide": place * 2 + 1 - core}, device_id_type=MESH)
    for other in others:
        pl.semaphore_signal(barrier, inc=1, device_id=other, device_id_type=MESH)

    @pl.when(place > 0)
    def _():
        pl.semaphore_signal(
            barrier, inc=1, device_id={"wide": (place - 1) * 2 + core}, device_id_type=MESH
        )

    @pl.when(place < PLACES - 1)
    def _():
        pl.semaphore_signal(
            barrier, inc=1, device_id={"wide": (place + 1) * 2 + core}, device_id_type=MESH
        )


def await_greetings(place, count):
    barrier = pltpu.get_barrier_semaphore()

    @pl.when((place == 0) | (place == PLACES - 1))
    def _():
        pl.semaphore_wait(barrier, count)

    @pl.when((place > 0) & (place < PLACES - 1))
    def _():
        pl.semaphore_wait(barrier, count + 1)


def ffn_ends(
    steps, hidden_ref, weight_ref, resid_hbm, own_ref, raw_hbm, marks_ref,
    sums, swapped, line, resid, stream, raw, acc,
    swap_sems, line_sems, cross_sems, raw_sems, resid_sem,
):
    wide_at = lax.axis_index("wide")
    section_at = lax.axis_index("section")
    place, core = wide_at // 2, wide_at % 2
    step = pl.program_id(0)
    rows, cols = sums.shape[4], sums.shape[5]
    last = PLACES - 1
    at_end = (place == 0) | (place == last)
    across = {"section": 1 - section_at}

    def fetch(kept):
        return pltpu.make_async_copy(resid_hbm.at[:, core, kept], resid, resid_sem)

    @pl.when(step == 0)
    def _():
        @pl.when(place == 0)
        def _():
            fetch(1).start()

        @pl.when(place == last)
        def _():
            fetch(0).start()

        greet(place, core, (across,))
        acc[...] = jnp.zeros_like(acc)

    def swap(way, i):
        return pltpu.make_async_remote_copy(
            src_ref=sums.at[i, 1 - core, way],
            dst_ref=swapped.at[i, way],
            send_sem=swap_sems.at[way, 0, i],
            recv_sem=swap_sems.at[way, 1, i],
            device_id={"wide": place * 2 + 1 - core},
            device_id_type=MESH,
        )

    def pass_on(way, i):
        towards = place + 1 if way == 0 else place - 1
        return pltpu.make_async_remote_copy(
            src_ref=line.at[way, i],
            dst_ref=line.at[way, i],
            send_sem=line_sems.at[way, 0, i],
            recv_sem=line_sems.at[way, 1, i],
            device_id={"wide": towards * 2 + core},
            device_id_type=MESH,
        )

    def columns(i):
        return pl.ds(pl.multiple_of(i * cols, cols), cols)

    def cross(i):
        return pltpu.make_async_remote_copy(
            src_ref=stream.at[:, :, columns(i)],
            dst_ref=raw.at[:, :, columns(i)],
            send_sem=cross_sems.at[0, i],
            recv_sem=cross_sems.at[1, i],
            device_id=across,
            device_id_type=MESH,
        )

    def store(i):
        return pltpu.make_async_copy(
            raw.at[:, :, columns(i)], raw_hbm.at[:, :, columns(i)], raw_sems.at[i]
        )

    @pl.when(step < steps)
    def _():
        result = lax.dot_general(
            hidden_ref[...], weight_ref[...], (((1,), (1,)), ((), ())), preferred_element_type=jnp.float32
        ).astype(jnp.bfloat16)
        for j in range(PLACES):
            part = result[4 * rows * j : 4 * rows * (j + 1)]
            sums[step, :, :, j] = part.reshape(2, 2, rows, cols)

        @pl.when(step == 0)
        def _():
            await_greetings(place, 3)

        for way in range(2):
            swap(way, step).start()

    for way in range(2):
        hops = place if way == 0 else last - place
        i = step - 1 - LAG * hops
        live = (i >= 0) & (i < steps)

        def mine(j):
            return sums[i, core, way, j].astype(jnp.float32) + swapped[i, way, j].astype(jnp.float32)

        @pl.when(live)
        def _():
            swap(way, i).wait_recv()

        @pl.when(live & (hops > 0))
        def _():
            pass_on(way, i).wait_recv()

        @pl.when(live & (hops == 0))
        def _():
            for j in range(PLACES):
                line[way, i, j] = mine(j).astype(jnp.bfloat16)

        @pl.when(live & (hops > 0) & (hops < last))
        def _():
            for j in range(PLACES):
                line[way, i, j] = (mine(j) + line[way, i, j].astype(jnp.float32)).astype(jnp.bfloat16)

        @pl.when(live & (hops < last))
        def _():
            pass_on(way, i).start()

        @pl.when(live & (hops == last))
        def _():
            @pl.when(i == 0)
            def _():
                fetch(way).wait()

            for j in range(PLACES):
                total = mine(j) + line[way, i, j].astype(jnp.float32)
                stream[j, :, columns(i)] = (
                    resid[j, :, columns(i)].astype(jnp.float32) + total
                ).astype(jnp.bfloat16)
            cross(i).start()

    came = step - 1 - LAG * last - CROSS_LAG

    @pl.when(at_end & (came >= 0) & (came < steps))
    def _():
        cross(came).wait_recv()
        store(came).start()
        for j in range(PLACES):
            values = raw[j, :, columns(came)].astype(jnp.float32)
            total, square = values[:, :LANES], values[:, :LANES] * values[:, :LANES]
            for at in range(LANES, cols, LANES):
                piece = values[:, at : at + LANES]
                total, square = total + piece, square + piece * piece
            acc[0, j] += total
            acc[1, j] += square

    @pl.when(step == steps + LAG * last + CROSS_LAG)
    def _():
        @pl.when(at_end)
        def _():
            lane = lax.broadcasted_iota(jnp.int32, (rows, LANES), 1)
            packed = jnp.zeros((rows, LANES), jnp.float32)
            for j in range(PLACES):
                for which in range(2):
                    total = jnp.sum(acc[which, j], axis=1, keepdims=True)
                    packed = jnp.where(lane == 2 * j + which, total, packed)
            marks_ref[...] = packed
            own_ref[...] = stream[place]

        def finish(i, carry):
            for way in range(2):
                hops = place if way == 0 else last - place
                swap(way, i).wait_send()

                @pl.when(hops < last)
                def _():
                    pass_on(way, i).wait_send()

            @pl.when(at_end)
            def _():
                cross(i).wait_send()
                store(i).wait()

            return carry

        lax.fori_loop(0, steps, finish, 0)


def ffn_rows(inner, down_weight, residual):
    seq_len, units = inner.shape
    width = down_weight.shape[0]
    cols = width // FFN_STEPS
    rows = seq_len // (4 * PLACES)
    last_step = FFN_STEPS - 1
    return pl.pallas_call(
        functools.partial(ffn_ends, FFN_STEPS),
        grid=(FFN_STEPS + LAG * (PLACES - 1) + CROSS_LAG + 1,),
        in_specs=[
            pl.BlockSpec((seq_len, units), lambda s: (0, 0), pipeline_mode=pl.Buffered(1)),
            pl.BlockSpec((cols, units), lambda s: (jnp.minimum(s, last_step), 0)),
            pl.BlockSpec(memory_space=pl.ANY),
        ],
        out_specs=[
            pl.BlockSpec((rows, width), lambda s: (0, 0), pipeline_mode=pl.Buffered(1)),
            pl.BlockSpec(memory_space=pl.ANY),
            pl.BlockSpec((rows, LANES), lambda s: (0, 0), pipeline_mode=pl.Buffered(1)),
        ],
        out_shape=[
            jax.ShapeDtypeStruct((rows, width), jnp.bfloat16),
            jax.ShapeDtypeStruct((PLACES, rows, width), jnp.bfloat16),
            jax.ShapeDtypeStruct((rows, LANES), jnp.float32),
        ],
        scratch_shapes=[
            pltpu.VMEM((FFN_STEPS, 2, 2, PLACES, rows, cols), jnp.bfloat16),
            pltpu.VMEM((FFN_STEPS, 2, PLACES, rows, cols), jnp.bfloat16),
            pltpu.VMEM((2, FFN_STEPS, PLACES, rows, cols), jnp.bfloat16),
            pltpu.VMEM((PLACES, rows, width), jnp.bfloat16),
            pltpu.VMEM((PLACES, rows, width), jnp.bfloat16),
            pltpu.VMEM((PLACES, rows, width), jnp.bfloat16),
            pltpu.VMEM((2, PLACES, rows, LANES), jnp.float32),
            pltpu.SemaphoreType.DMA((2, 2, FFN_STEPS)),
            pltpu.SemaphoreType.DMA((2, 2, FFN_STEPS)),
            pltpu.SemaphoreType.DMA((2, FFN_STEPS)),
            pltpu.SemaphoreType.DMA((FFN_STEPS,)),
            pltpu.SemaphoreType.DMA,
        ],
        compiler_params=pltpu.CompilerParams(
            collective_id=0, has_side_effects=True, vmem_limit_bytes=60 << 20
        ),
        cost_estimate=pl.CostEstimate(
            flops=2 * seq_len * units * width, bytes_accessed=2 * units * width, transcendentals=0
        ),
    )(inner, down_weight, residual.reshape(PLACES, 2, 2, rows, width))


def qkv_attend(
    raw_hbm, sums_in, own_hbm, gain_ref, bias_ref, weight_hbm, out_hbm, mine_hbm,
    line, marks, parts, rows_of, weight, sending, coming, joined, attended,
    part_sems, weight_sem, raw_sem, own_sem, mark_sems, line_sems, share_sems, back_sems, swap_sems, out_sems,
    free_sems,
):
    wide_at = lax.axis_index("wide")
    section_at = lax.axis_index("section")
    narrow_at = lax.axis_index("narrow")
    place, core = wide_at // 2, wide_at % 2
    last = PLACES - 1
    tiles, tile_rows, tile_cols = sending.shape[2:]
    half = tiles * tile_cols
    rows, depth = rows_of.shape[3:]
    cols = depth // PIECES
    pieces = PLACES * PIECES
    heads = attended.shape[1]
    across = {"section": 1 - section_at}
    partner = {"narrow": 1 - narrow_at}
    twin = {"wide": place * 2 + 1 - core}

    fetch = pltpu.make_async_copy(weight_hbm, weight, weight_sem)

    def begin(kept):
        return pltpu.make_async_copy(raw_hbm, line.at[kept], raw_sem)

    def settle(kept):
        return pltpu.make_async_copy(own_hbm, mine_hbm.at[pl.ds(kept * rows, rows)], own_sem)

    def at_source(kept):
        return place == (last if kept == 0 else 0)

    for kept in range(2):

        @pl.when(at_source(kept))
        def _():
            begin(kept).start()
            settle(kept).start()
            parts[0] = sums_in[...]

    fetch.start()
    greet(place, core, (across, partner))
    await_greetings(place, 4)
    add_up = pltpu.make_async_remote_copy(
        src_ref=parts.at[0],
        dst_ref=parts.at[1],
        send_sem=part_sems.at[0],
        recv_sem=part_sems.at[1],
        device_id=partner,
        device_id_type=MESH,
    )
    for kept in range(2):

        @pl.when(at_source(kept))
        def _():
            add_up.start()
            begin(kept).wait()

    def onwards(way):
        return {"wide": (place - 1 if way == 0 else place + 1) * 2 + core}

    def columns(q):
        return pl.ds(pl.multiple_of(q * cols, cols), cols)

    def pass_marks(way):
        return pltpu.make_async_remote_copy(
            src_ref=marks.at[way],
            dst_ref=marks.at[way],
            send_sem=mark_sems.at[way, 0],
            recv_sem=mark_sems.at[way, 1],
            device_id=onwards(way),
            device_id_type=MESH,
        )

    def pass_on(way, i):
        part = line.at[way, i // PIECES, :, columns(i % PIECES)]
        return pltpu.make_async_remote_copy(
            src_ref=part,
            dst_ref=part,
            send_sem=line_sems.at[way, 0, i],
            recv_sem=line_sems.at[way, 1, i],
            device_id=onwards(way),
            device_id_type=MESH,
        )

    def give_back(way, q):
        return pltpu.make_async_remote_copy(
            src_ref=line.at[way, place, :, columns(q)],
            dst_ref=mine_hbm.at[pl.ds(way * rows, rows), columns(q)],
            send_sem=back_sems.at[way, 0, q],
            recv_sem=back_sems.at[way, 1, q],
            device_id=across,
            device_id_type=MESH,
        )

    def share(way, i):
        part = rows_of.at[(i // PIECES) % 2, way, core, :, columns(i % PIECES)]
        return pltpu.make_async_remote_copy(
            src_ref=part,
            dst_ref=part,
            send_sem=share_sems.at[way, 0, i],
            recv_sem=share_sems.at[way, 1, i],
            device_id=twin,
            device_id_type=MESH,
        )

    def swap(way, phase, tile):
        return pltpu.make_async_remote_copy(
            src_ref=sending.at[way, phase, tile],
            dst_ref=coming.at[way, phase, tile],
            send_sem=swap_sems.at[way, 0, phase, tile],
            recv_sem=swap_sems.at[way, 1, phase, tile],
            device_id=partner,
            device_id_type=MESH,
        )

    def into(block, head):
        row = pl.ds((block % 2) * 4 * rows, 4 * rows)
        column = pl.ds(pl.multiple_of((narrow_at * heads + head) * HDIM, HDIM), HDIM)
        return out_hbm.at[row, column]

    def deliver(block, head):
        return pltpu.make_async_remote_copy(
            src_ref=attended.at[block, head],
            dst_ref=into(block, head),
            send_sem=out_sems.at[0, block % 2, head],
            recv_sem=out_sems.at[1, block % 2, head],
            device_id=partner,
            device_id_type=MESH,
        )

    def keep(block, head):
        return pltpu.make_async_copy(
            attended.at[block, head], into(block, head), out_sems.at[2, block % 2, head]
        )

    def hops_of(way):
        return last - place if way == 0 else place

    def tile_at(tile):
        return pl.ds(pl.multiple_of(tile * tile_cols, tile_cols), tile_cols)

    def arrive(way, n):
        hops = hops_of(way)
        i = n - LAG * hops
        phase, q = i // PIECES, i % PIECES

        @pl.when((i >= 0) & (i < pieces))
        def _():
            @pl.when(hops > 0)
            def _():
                pass_on(way, i).wait_recv()

            @pl.when(hops < last)
            def _():
                pass_on(way, i).start()

            @pl.when(i == 0)
            def _():
                @pl.when(hops == 0)
                def _():
                    add_up.wait()
                    full = (parts[0] + parts[1]) / D
                    lane = lax.broadcasted_iota(jnp.int32, (rows, LANES), 1)
                    both = jnp.zeros((rows, LANES), jnp.float32)
                    for j in range(PLACES):
                        mean = full[:, 2 * j : 2 * j + 1]
                        var = full[:, 2 * j + 1 : 2 * j + 2] - mean * mean
                        both = jnp.where(lane == 2 * j, mean, both)
                        both = jnp.where(lane == 2 * j + 1, lax.rsqrt(var + 1e-05), both)
                    marks[way] = both

                @pl.when(hops > 0)
                def _():
                    pass_marks(way).wait_recv()

                @pl.when(hops < last)
                def _():
                    pass_marks(way).start()

            @pl.when((hops > 0) & (phase == place))
            def _():
                give_back(way, q).start()

            @pl.when((phase >= 2) & (q == 0))
            def _():
                pl.semaphore_wait(free_sems.at[way], 1)

            @pl.when(phase >= 2)
            def _():
                share(way, i - 2 * PIECES).wait_send()

            lane = lax.broadcasted_iota(jnp.int32, (rows, LANES), 1)
            at = columns(q)
            both = marks[way]
            mean = jnp.sum(jnp.where(lane == 2 * phase, both, 0.0), axis=1, keepdims=True)
            rstd = jnp.sum(jnp.where(lane == 2 * phase + 1, both, 0.0), axis=1, keepdims=True)
            values = line[way, phase, :, at].astype(jnp.float32)
            rows_of[phase % 2, way, core, :, at] = (
                (values - mean) * rstd * gain_ref[:, at] + bias_ref[:, at]
            ).astype(jnp.bfloat16)
            share(way, i).start()

    def project(way, n):
        d = n - LAG * hops_of(way) - PIECES
        phase, tile = d // PIECES, d % PIECES

        @pl.when((d >= 0) & (d < pieces))
        def _():
            @pl.when(tile == 0)
            def _():
                def arrived(q, carry):
                    share(way, phase * PIECES + q).wait_recv()
                    return carry

                lax.fori_loop(0, PIECES, arrived, 0)

            away = tile < tiles
            column = jnp.where(
                away,
                (1 - narrow_at) * half + tile * tile_cols,
                narrow_at * half + (tile - tiles) * tile_cols,
            )
            product = lax.dot_general(
                rows_of[phase % 2, way].reshape(tile_rows, depth),
                weight[:, pl.ds(pl.multiple_of(column, tile_cols), tile_cols)],
                (((1,), (0,)), ((), ())),
                preferred_element_type=jnp.float32,
            ).astype(jnp.bfloat16)

            @pl.when(away)
            def _():
                sending[way, phase, tile] = product
                swap(way, phase, tile).start()

            @pl.when(tile >= tiles)
            def _():
                for which in range(2):
                    at = pl.ds((2 * which + way) * rows, rows)
                    joined[phase, at, tile_at(tile - tiles)] = product[which * rows : (which + 1) * rows]

            @pl.when((tile == PIECES - 1) & (phase < PLACES - 2))
            def _():
                pl.semaphore_signal(free_sems.at[way], inc=1, device_id=twin, device_id_type=MESH)

        t = d - tiles - TAKE_LAG
        taken, of = t // PIECES, t % PIECES

        @pl.when((t >= 0) & (t < pieces) & (of < tiles))
        def _():
            swap(way, taken, of).wait_recv()
            for which in range(2):
                at = pl.ds((2 * which + way) * rows, rows)
                came = coming[way, taken, of, which * rows : (which + 1) * rows].astype(jnp.float32)
                both = joined[taken, at, tile_at(of)].astype(jnp.float32) + came
                joined[taken, at, tile_at(of)] = both.astype(jnp.bfloat16)

    whole = LAG * jnp.maximum(place, last - place) + PIECES + 2 * tiles + TAKE_LAG

    def tick(n, carry):
        for way in range(2):
            arrive(way, n)

        @pl.when(n == PIECES)
        def _():
            fetch.wait()

        for way in range(2):
            project(way, n)

        a = n - whole
        head = a % PIECES
        for block in range(PLACES):

            @pl.when((a // PIECES == block) & (head < heads) & (a >= 0))
            def _():
                attended[block, head] = attend_block(joined, head, block)

                @pl.when(narrow_at == block // 2)
                def _():
                    keep(block, head).start()

                if block >= PLACES // 2:

                    @pl.when(narrow_at != block // 2)
                    def _():
                        deliver(block, head).start()

        @pl.when((n == LAG * last + pieces + tiles) & (narrow_at == 1))
        def _():
            for block in range(PLACES // 2):
                for head in range(heads):
                    deliver(block, head).start()

        return carry

    lax.fori_loop(0, LAG * last + PIECES + 2 * tiles + TAKE_LAG + (PLACES - 1) * PIECES + heads, tick, 0)

    def finish(i, carry):
        for way in range(2):

            @pl.when(i >= 2 * PIECES)
            def _():
                share(way, i).wait_send()

            @pl.when(hops_of(way) < last)
            def _():
                pass_on(way, i).wait_send()

        return carry

    lax.fori_loop(0, pieces, finish, 0)

    for way in range(2):

        @pl.when(hops_of(way) < last)
        def _():
            pass_marks(way).wait_send()

        @pl.when(hops_of(way) > 0)
        def _():
            for q in range(PIECES):
                give_back(way, q).wait()

        @pl.when(at_source(way))
        def _():
            settle(way).wait()

        for phase in range(PLACES):
            for tile in range(tiles):
                swap(way, phase, tile).wait_send()

    for block in range(2):
        for head in range(heads):
            deliver(block, head).wait()
            keep(block, head).wait()


def qkv_rows(raw, marks, own, gain, bias, qkv_weight):
    rows, depth = raw.shape[1:]
    width = qkv_weight.shape[1]
    half = width // 2
    tiles = PIECES // 2
    heads = half // (3 * HDIM)
    passed = (2, PLACES, tiles, 2 * rows, half // tiles)
    pieces = PLACES * PIECES
    seq_len = 4 * PLACES * rows
    vmem = pl.BlockSpec(memory_space=pltpu.VMEM)
    hbm = pl.BlockSpec(memory_space=pl.ANY)
    return pl.pallas_call(
        qkv_attend,
        in_specs=[hbm, vmem, hbm, vmem, vmem, hbm],
        out_specs=[hbm, hbm],
        out_shape=[
            jax.ShapeDtypeStruct((seq_len // 2, 2 * heads * HDIM), jnp.bfloat16),
            jax.ShapeDtypeStruct((2 * rows, depth), jnp.bfloat16),
        ],
        scratch_shapes=[
            pltpu.VMEM((2, PLACES, rows, depth), jnp.bfloat16),
            pltpu.VMEM((2, rows, LANES), jnp.float32),
            pltpu.VMEM((2, rows, LANES), jnp.float32),
            pltpu.VMEM((2, 2, 2, rows, depth), jnp.bfloat16),
            pltpu.VMEM((depth, width), jnp.bfloat16),
            pltpu.VMEM(passed, jnp.bfloat16),
            pltpu.VMEM(passed, jnp.bfloat16),
            pltpu.VMEM((PLACES, 4 * rows, half), jnp.bfloat16),
            pltpu.VMEM((PLACES, heads, 4 * rows, HDIM), jnp.bfloat16),
            pltpu.SemaphoreType.DMA((2,)),
            pltpu.SemaphoreType.DMA,
            pltpu.SemaphoreType.DMA,
            pltpu.SemaphoreType.DMA,
            pltpu.SemaphoreType.DMA((2, 2)),
            pltpu.SemaphoreType.DMA((2, 2, pieces)),
            pltpu.SemaphoreType.DMA((2, 2, pieces)),
            pltpu.SemaphoreType.DMA((2, 2, PIECES)),
            pltpu.SemaphoreType.DMA((2, 2, PLACES, tiles)),
            pltpu.SemaphoreType.DMA((3, 2, heads)),
            pltpu.SemaphoreType.REGULAR((2,)),
        ],
        compiler_params=pltpu.CompilerParams(
            collective_id=1, has_side_effects=True, vmem_limit_bytes=63 << 20
        ),
        cost_estimate=pl.CostEstimate(
            flops=2 * seq_len * depth * width + 3 * heads * seq_len * seq_len * HDIM,
            bytes_accessed=2 * depth * width,
            transcendentals=heads * seq_len * seq_len // 2,
        ),
    )(raw, marks, own, gain, bias, qkv_weight)


def copy_both(attended_hbm, mine_hbm, out_hbm, stream_hbm, attended, mine, sems):
    steps = []
    pairs = ((mine_hbm, mine, stream_hbm), (attended_hbm, attended, out_hbm))
    for which, (source, held, target) in enumerate(pairs):
        rows = source.shape[0] // COPIES
        for part in range(COPIES):
            at = pl.ds(part * rows, rows)
            load = pltpu.make_async_copy(source.at[at], held.at[at], sems.at[0, which, part])
            store = pltpu.make_async_copy(held.at[at], target.at[at], sems.at[1, which, part])
            steps.append((load, store))
    for load, _ in steps:
        load.start()
    for load, store in steps:
        load.wait()
        store.start()
    for _, store in steps:
        store.wait()


def hand_over(attended, mine):
    hbm = pl.BlockSpec(memory_space=pl.ANY)
    return pl.pallas_call(
        copy_both,
        in_specs=[hbm, hbm],
        out_specs=[hbm, hbm],
        out_shape=[jax.ShapeDtypeStruct(a.shape, a.dtype) for a in (attended, mine)],
        scratch_shapes=[
            pltpu.VMEM(attended.shape, attended.dtype),
            pltpu.VMEM(mine.shape, mine.dtype),
            pltpu.SemaphoreType.DMA((2, 2, COPIES)),
        ],
        compiler_params=pltpu.CompilerParams(vmem_limit_bytes=62 << 20),
    )(attended, mine)


def split_heads(hidden, down_weight, residual, ln_gain, ln_bias, qkv_weight):
    own, raw, marks = ffn_rows(hidden[0], down_weight, residual[0])
    attended, mine = qkv_rows(raw, marks, own, ln_gain[None], ln_bias[None], qkv_weight)
    attended, mine = hand_over(attended, mine)
    return (mine[None], attended[None])


def split_queries(hidden, down_weight, residual, ln_gain, ln_bias, qkv_weight):
    inner = hidden[0]
    resid = residual[0]
    seq_len = inner.shape[0]
    wide_rows = seq_len // lax.axis_size("wide")
    wide_at = lax.axis_index("wide")
    contract = (((1,), (1,)), ((), ()))
    partial_ffn = lax.dot_general(inner, down_weight, contract, preferred_element_type=jnp.float32)
    summed = lax.psum(partial_ffn, "wide")
    mine = (resid.astype(jnp.float32) + summed).astype(jnp.bfloat16)
    arrived = from_behind(mine, "section", 1)
    own_rows = lax.dynamic_slice_in_dim(mine, wide_at * wide_rows, wide_rows, 0)
    values = arrived.astype(jnp.float32)
    totals, squares = lax.psum(
        (jnp.sum(values, axis=1), jnp.sum(values * values, axis=1)), "narrow"
    )
    mean = totals / D
    var = squares / D - mean * mean
    normed = (
        (values - mean[:, None]) * lax.rsqrt(var + 1e-05)[:, None] * ln_gain + ln_bias
    ).astype(jnp.bfloat16)
    heads_here = qkv_weight.shape[1] // (3 * HDIM)
    query_count = seq_len // lax.axis_size("narrow")
    narrow_at = lax.axis_index("narrow")
    joined = lax.psum(
        jnp.dot(normed, qkv_weight, preferred_element_type=jnp.float32), "narrow"
    ).astype(jnp.bfloat16)
    mine_joined = lax.dynamic_slice_in_dim(joined, narrow_at * query_count, query_count, 0)
    query = mine_joined.reshape(query_count, heads_here, 3, HDIM)[:, :, 0]
    pairs = joined.reshape(seq_len, heads_here, 3, HDIM)[:, :, 1:]
    keys = pairs[:, :, 0]
    vals = pairs[:, :, 1]
    scores = jnp.einsum("qhd,khd->hqk", query, keys, preferred_element_type=jnp.float32) / jnp.sqrt(
        jnp.float32(HDIM)
    )
    query_pos = narrow_at * query_count + lax.broadcasted_iota(jnp.int32, (query_count, seq_len), 0)
    key_pos = lax.broadcasted_iota(jnp.int32, (query_count, seq_len), 1)
    scores = jnp.where((key_pos <= query_pos)[None], scores, jnp.float32(-1e30))
    top = jnp.max(scores, axis=2, keepdims=True)
    expd = jnp.exp(scores - top)
    probs = (expd / jnp.sum(expd, axis=2, keepdims=True)).astype(jnp.bfloat16)
    attended = jnp.einsum("hqk,khd->qhd", probs, vals, preferred_element_type=jnp.float32).astype(
        jnp.bfloat16
    )
    attended = attended.reshape(query_count, heads_here * HDIM)
    return (own_rows[None], attended[None])


def per_device(hidden, down_weight, residual, ln_gain, ln_bias, qkv_weight):
    heads_here = qkv_weight.shape[1] // (3 * HDIM)
    wide_rows = hidden.shape[1] // lax.axis_size("wide")
    even = heads_here % 8 == 0 and wide_rows % 32 == 0
    line = lax.axis_size("section") == 2 and lax.axis_size("wide") == 2 * PLACES and lax.axis_size("narrow") == 2
    even = even and down_weight.shape[0] % (FFN_STEPS * 128) == 0
    plan = split_heads if line and even else split_queries
    return plan(hidden, down_weight, residual, ln_gain, ln_bias, qkv_weight)


def solution(mesh):
    return jax.shard_map(
        per_device,
        mesh=mesh,
        in_specs=(
            P("section", None, "wide"),
            P("narrow", "wide"),
            P("section", None, "narrow"),
            P("narrow"),
            P("narrow"),
            P("narrow", "wide"),
        ),
        out_specs=(P("section", "wide", "narrow"), P("section", "narrow", "wide")),
        check_vma=False,
    )
```

```python
import functools

import jax
import jax.numpy as jnp
from jax import lax
from jax.experimental import pallas as pl
from jax.experimental.pallas import tpu as pltpu
from jax.sharding import PartitionSpec as P

D = 12288
HDIM = 128
LANES = 128
PLACES = 4
FFN_STEPS = 24
PIECES = 6
LAG = 2
TAKE_LAG = 3
SENT_LAG = 2
SWAP_LAG = 3
COPIES = 4
MESH = pl.DeviceIdType.MESH


def from_behind(value, axis, steps):
    count = lax.axis_size(axis)
    pairs = [(source, (source + steps) % count) for source in range(count)]
    return lax.ppermute(value, axis, pairs)


def attend_block(joined_ref, head, block):
    factor = 1.4426950408889634 / (HDIM**0.5)
    size = joined_ref.shape[1]

    def part(which):
        return pl.ds(pl.multiple_of((3 * head + which) * HDIM, HDIM), HDIM)

    def scores_of(keys):
        return lax.dot_general(query, keys, (((1,), (1,)), ((), ())), preferred_element_type=jnp.float32)

    query = joined_ref[block, :, part(0)]
    shape = (size, size)
    seen = lax.broadcasted_iota(jnp.int32, shape, 1) <= lax.broadcasted_iota(jnp.int32, shape, 0)
    near = jnp.where(seen, scores_of(joined_ref[block, :, part(1)]), jnp.float32(-1e30))
    top = jnp.max(near, axis=1, keepdims=True)
    if block:
        far = scores_of(joined_ref[:block, :, part(1)].reshape(block * size, HDIM))
        top = jnp.maximum(top, jnp.max(far, axis=1, keepdims=True))
    near = jnp.exp2((near - top) * factor)
    total = jnp.sum(near, axis=1, keepdims=True)
    out = jnp.dot(
        near.astype(jnp.bfloat16), joined_ref[block, :, part(2)], preferred_element_type=jnp.float32
    )
    if block:
        far = jnp.exp2((far - top) * factor)
        total += jnp.sum(far, axis=1, keepdims=True)
        out += jnp.dot(
            far.astype(jnp.bfloat16),
            joined_ref[:block, :, part(2)].reshape(block * size, HDIM),
            preferred_element_type=jnp.float32,
        )
    return (out * (1.0 / total)).astype(jnp.bfloat16)


def greet(place, core, others):
    barrier = pltpu.get_barrier_semaphore()
    pl.semaphore_signal(barrier, inc=1, device_id={"wide": place * 2 + 1 - core}, device_id_type=MESH)
    for other in others:
        pl.semaphore_signal(barrier, inc=1, device_id=other, device_id_type=MESH)

    @pl.when(place > 0)
    def _():
        pl.semaphore_signal(
            barrier, inc=1, device_id={"wide": (place - 1) * 2 + core}, device_id_type=MESH
        )

    @pl.when(place < PLACES - 1)
    def _():
        pl.semaphore_signal(
            barrier, inc=1, device_id={"wide": (place + 1) * 2 + core}, device_id_type=MESH
        )


def await_greetings(place, count):
    barrier = pltpu.get_barrier_semaphore()

    @pl.when((place == 0) | (place == PLACES - 1))
    def _():
        pl.semaphore_wait(barrier, count)

    @pl.when((place > 0) & (place < PLACES - 1))
    def _():
        pl.semaphore_wait(barrier, count + 1)


def ffn_ends(
    steps, hidden_ref, weight_ref, resid_hbm, own_hbm, raw_hbm, sums_ref,
    sums, swapped, line, resid, stream, acc, parts,
    swap_sems, line_sems, cross_sems, own_sems, resid_sem, part_sems,
):
    wide_at = lax.axis_index("wide")
    section_at = lax.axis_index("section")
    place, core = wide_at // 2, wide_at % 2
    step = pl.program_id(0)
    rows, cols = sums.shape[4], sums.shape[5]
    last = PLACES - 1
    at_end = (place == 0) | (place == last)
    across = {"section": 1 - section_at}

    def fetch(kept):
        return pltpu.make_async_copy(resid_hbm.at[:, core, kept], resid, resid_sem)

    @pl.when(step == 0)
    def _():
        @pl.when(place == 0)
        def _():
            fetch(1).start()

        @pl.when(place == last)
        def _():
            fetch(0).start()

        greet(place, core, (across,))
        acc[...] = jnp.zeros_like(acc)

    def swap(way, i):
        return pltpu.make_async_remote_copy(
            src_ref=sums.at[i, 1 - core, way],
            dst_ref=swapped.at[i, way],
            send_sem=swap_sems.at[way, 0, i],
            recv_sem=swap_sems.at[way, 1, i],
            device_id={"wide": place * 2 + 1 - core},
            device_id_type=MESH,
        )

    def pass_on(way, i):
        towards = place + 1 if way == 0 else place - 1
        return pltpu.make_async_remote_copy(
            src_ref=line.at[way, i],
            dst_ref=line.at[way, i],
            send_sem=line_sems.at[way, 0, i],
            recv_sem=line_sems.at[way, 1, i],
            device_id={"wide": towards * 2 + core},
            device_id_type=MESH,
        )

    def columns(i):
        return pl.ds(pl.multiple_of(i * cols, cols), cols)

    def cross(i):
        return pltpu.make_async_remote_copy(
            src_ref=stream.at[:, :, columns(i)],
            dst_ref=raw_hbm.at[:, :, columns(i)],
            send_sem=cross_sems.at[0, i],
            recv_sem=cross_sems.at[1, i],
            device_id=across,
            device_id_type=MESH,
        )

    def store(i):
        return pltpu.make_async_copy(
            stream.at[place, :, columns(i)], own_hbm.at[:, columns(i)], own_sems.at[i]
        )

    @pl.when(step < steps)
    def _():
        result = lax.dot_general(
            hidden_ref[...], weight_ref[...], (((1,), (1,)), ((), ())), preferred_element_type=jnp.float32
        ).astype(jnp.bfloat16)
        for j in range(PLACES):
            part = result[4 * rows * j : 4 * rows * (j + 1)]
            sums[step, :, :, j] = part.reshape(2, 2, rows, cols)

        @pl.when(step == 0)
        def _():
            await_greetings(place, 3)

        for way in range(2):
            swap(way, step).start()

    for way in range(2):
        hops = place if way == 0 else last - place
        i = step - 1 - LAG * hops
        live = (i >= 0) & (i < steps)

        def mine(j):
            return sums[i, core, way, j].astype(jnp.float32) + swapped[i, way, j].astype(jnp.float32)

        sent = i - SENT_LAG

        @pl.when((sent >= 0) & (sent < steps) & (hops < last))
        def _():
            pass_on(way, sent).wait_send()

        @pl.when((sent >= 0) & (hops == last))
        def _():
            cross(sent).wait()
            store(sent).wait()

        @pl.when((step >= SWAP_LAG) & (step < steps + SWAP_LAG))
        def _():
            swap(way, step - SWAP_LAG).wait_send()

        @pl.when(live)
        def _():
            swap(way, i).wait_recv()

        @pl.when(live & (hops > 0))
        def _():
            pass_on(way, i).wait_recv()

        @pl.when(live & (hops == 0))
        def _():
            for j in range(PLACES):
                line[way, i, j] = mine(j).astype(jnp.bfloat16)

        @pl.when(live & (hops > 0) & (hops < last))
        def _():
            for j in range(PLACES):
                line[way, i, j] = (mine(j) + line[way, i, j].astype(jnp.float32)).astype(jnp.bfloat16)

        @pl.when(live & (hops < last))
        def _():
            pass_on(way, i).start()

        @pl.when(live & (hops == last))
        def _():
            @pl.when(i == 0)
            def _():
                fetch(way).wait()

            for j in range(PLACES):
                total = mine(j) + line[way, i, j].astype(jnp.float32)
                rounded = (resid[j, :, columns(i)].astype(jnp.float32) + total).astype(jnp.bfloat16)
                stream[j, :, columns(i)] = rounded
                values = rounded.astype(jnp.float32)
                for at in range(0, cols, LANES):
                    piece = values[:, at : at + LANES]
                    acc[0, j] += piece
                    acc[1, j] += piece * piece
            cross(i).start()
            store(i).start()

    @pl.when(step == steps + LAG * last)
    def _():
        @pl.when(at_end)
        def _():
            lane = lax.broadcasted_iota(jnp.int32, (rows, LANES), 1)
            packed = jnp.zeros((rows, LANES), jnp.float32)
            for j in range(PLACES):
                for which in range(2):
                    total = jnp.sum(acc[which, j], axis=1, keepdims=True)
                    packed = jnp.where(lane == 2 * j + which, total, packed)
            parts[0] = packed
            give = pltpu.make_async_remote_copy(
                src_ref=parts.at[0],
                dst_ref=parts.at[1],
                send_sem=part_sems.at[0],
                recv_sem=part_sems.at[1],
                device_id=across,
                device_id_type=MESH,
            )
            give.start()
            give.wait()
            sums_ref[...] = parts[1]

        @pl.when(at_end)
        def _():
            for i in range(steps - SENT_LAG, steps):
                cross(i).wait()
                store(i).wait()


def ffn_rows(inner, down_weight, residual):
    seq_len, units = inner.shape
    width = down_weight.shape[0]
    cols = width // FFN_STEPS
    rows = seq_len // (4 * PLACES)
    last_step = FFN_STEPS - 1
    return pl.pallas_call(
        functools.partial(ffn_ends, FFN_STEPS),
        grid=(FFN_STEPS + LAG * (PLACES - 1) + 1,),
        in_specs=[
            pl.BlockSpec((seq_len, units), lambda s: (0, 0), pipeline_mode=pl.Buffered(1)),
            pl.BlockSpec((cols, units), lambda s: (jnp.minimum(s, last_step), 0)),
            pl.BlockSpec(memory_space=pl.ANY),
        ],
        out_specs=[
            pl.BlockSpec(memory_space=pl.ANY),
            pl.BlockSpec(memory_space=pl.ANY),
            pl.BlockSpec((rows, LANES), lambda s: (0, 0), pipeline_mode=pl.Buffered(1)),
        ],
        out_shape=[
            jax.ShapeDtypeStruct((rows, width), jnp.bfloat16),
            jax.ShapeDtypeStruct((PLACES, rows, width), jnp.bfloat16),
            jax.ShapeDtypeStruct((rows, LANES), jnp.float32),
        ],
        scratch_shapes=[
            pltpu.VMEM((FFN_STEPS, 2, 2, PLACES, rows, cols), jnp.bfloat16),
            pltpu.VMEM((FFN_STEPS, 2, PLACES, rows, cols), jnp.bfloat16),
            pltpu.VMEM((2, FFN_STEPS, PLACES, rows, cols), jnp.bfloat16),
            pltpu.VMEM((PLACES, rows, width), jnp.bfloat16),
            pltpu.VMEM((PLACES, rows, width), jnp.bfloat16),
            pltpu.VMEM((2, PLACES, rows, LANES), jnp.float32),
            pltpu.VMEM((2, rows, LANES), jnp.float32),
            pltpu.SemaphoreType.DMA((2, 2, FFN_STEPS)),
            pltpu.SemaphoreType.DMA((2, 2, FFN_STEPS)),
            pltpu.SemaphoreType.DMA((2, FFN_STEPS)),
            pltpu.SemaphoreType.DMA((FFN_STEPS,)),
            pltpu.SemaphoreType.DMA,
            pltpu.SemaphoreType.DMA((2,)),
        ],
        compiler_params=pltpu.CompilerParams(
            collective_id=0, has_side_effects=True, vmem_limit_bytes=60 << 20
        ),
        cost_estimate=pl.CostEstimate(
            flops=2 * seq_len * units * width, bytes_accessed=2 * units * width, transcendentals=0
        ),
    )(inner, down_weight, residual.reshape(PLACES, 2, 2, rows, width))


def qkv_attend(
    raw_hbm, sums_in, own_hbm, gain_ref, bias_ref, weight_hbm, out_hbm, mine_hbm,
    line, marks, parts, rows_of, weight, sending, coming, joined, attended,
    part_sems, weight_sem, raw_sems, own_sem, mark_sems, line_sems, share_sems, back_sems, swap_sems, out_sems,
    free_sems,
):
    wide_at = lax.axis_index("wide")
    section_at = lax.axis_index("section")
    narrow_at = lax.axis_index("narrow")
    place, core = wide_at // 2, wide_at % 2
    last = PLACES - 1
    tiles, tile_rows, tile_cols = sending.shape[2:]
    half = tiles * tile_cols
    rows, depth = rows_of.shape[3:]
    cols = depth // PIECES
    pieces = PLACES * PIECES
    heads = attended.shape[1]
    across = {"section": 1 - section_at}
    partner = {"narrow": 1 - narrow_at}
    twin = {"wide": place * 2 + 1 - core}

    fetch = pltpu.make_async_copy(weight_hbm, weight, weight_sem)

    def begin(kept, j):
        return pltpu.make_async_copy(raw_hbm.at[j], line.at[kept, j], raw_sems.at[j])

    def settle(kept):
        return pltpu.make_async_copy(own_hbm, mine_hbm.at[pl.ds(kept * rows, rows)], own_sem)

    def at_source(kept):
        return place == (last if kept == 0 else 0)

    for kept in range(2):

        @pl.when(at_source(kept))
        def _():
            for j in range(PLACES):
                begin(kept, j).start()
            parts[0] = sums_in[...]

    fetch.start()
    greet(place, core, (across, partner))
    await_greetings(place, 4)
    add_up = pltpu.make_async_remote_copy(
        src_ref=parts.at[0],
        dst_ref=parts.at[1],
        send_sem=part_sems.at[0],
        recv_sem=part_sems.at[1],
        device_id=partner,
        device_id_type=MESH,
    )
    for kept in range(2):

        @pl.when(at_source(kept))
        def _():
            add_up.start()
            settle(kept).start()

    def onwards(way):
        return {"wide": (place - 1 if way == 0 else place + 1) * 2 + core}

    def columns(q):
        return pl.ds(pl.multiple_of(q * cols, cols), cols)

    def pass_marks(way):
        return pltpu.make_async_remote_copy(
            src_ref=marks.at[way],
            dst_ref=marks.at[way],
            send_sem=mark_sems.at[way, 0],
            recv_sem=mark_sems.at[way, 1],
            device_id=onwards(way),
            device_id_type=MESH,
        )

    def pass_on(way, i):
        part = line.at[way, i // PIECES, :, columns(i % PIECES)]
        return pltpu.make_async_remote_copy(
            src_ref=part,
            dst_ref=part,
            send_sem=line_sems.at[way, 0, i],
            recv_sem=line_sems.at[way, 1, i],
            device_id=onwards(way),
            device_id_type=MESH,
        )

    def give_back(way, q):
        return pltpu.make_async_remote_copy(
            src_ref=line.at[way, place, :, columns(q)],
            dst_ref=mine_hbm.at[pl.ds(way * rows, rows), columns(q)],
            send_sem=back_sems.at[way, 0, q],
            recv_sem=back_sems.at[way, 1, q],
            device_id=across,
            device_id_type=MESH,
        )

    def share(way, i):
        part = rows_of.at[(i // PIECES) % 2, way, core, :, columns(i % PIECES)]
        return pltpu.make_async_remote_copy(
            src_ref=part,
            dst_ref=part,
            send_sem=share_sems.at[way, 0, i],
            recv_sem=share_sems.at[way, 1, i],
            device_id=twin,
            device_id_type=MESH,
        )

    def swap(way, phase, tile):
        return pltpu.make_async_remote_copy(
            src_ref=sending.at[way, phase, tile],
            dst_ref=coming.at[way, phase, tile],
            send_sem=swap_sems.at[way, 0, phase, tile],
            recv_sem=swap_sems.at[way, 1, phase, tile],
            device_id=partner,
            device_id_type=MESH,
        )

    def into(block, head):
        row = pl.ds((block % 2) * 4 * rows, 4 * rows)
        column = pl.ds(pl.multiple_of((narrow_at * heads + head) * HDIM, HDIM), HDIM)
        return out_hbm.at[row, column]

    def deliver(block, head):
        return pltpu.make_async_remote_copy(
            src_ref=attended.at[block, head],
            dst_ref=into(block, head),
            send_sem=out_sems.at[0, block % 2, head],
            recv_sem=out_sems.at[1, block % 2, head],
            device_id=partner,
            device_id_type=MESH,
        )

    def keep(block, head):
        return pltpu.make_async_copy(
            attended.at[block, head], into(block, head), out_sems.at[2, block % 2, head]
        )

    def hops_of(way):
        return last - place if way == 0 else place

    def tile_at(tile):
        return pl.ds(pl.multiple_of(tile * tile_cols, tile_cols), tile_cols)

    def arrive(way, n):
        hops = hops_of(way)
        i = n - LAG * hops
        phase, q = i // PIECES, i % PIECES
        sent = i - SENT_LAG

        @pl.when((sent >= 0) & (sent < pieces))
        def _():
            share(way, sent).wait_send()

            @pl.when(hops < last)
            def _():
                pass_on(way, sent).wait_send()

        @pl.when((i >= 0) & (i < pieces))
        def _():
            @pl.when((hops == 0) & (q == 0))
            def _():
                begin(way, phase).wait()

            @pl.when(hops > 0)
            def _():
                pass_on(way, i).wait_recv()

            @pl.when(hops < last)
            def _():
                pass_on(way, i).start()

            @pl.when(i == 0)
            def _():
                @pl.when(hops == 0)
                def _():
                    add_up.wait()
                    full = (parts[0] + parts[1]) / D
                    lane = lax.broadcasted_iota(jnp.int32, (rows, LANES), 1)
                    both = jnp.zeros((rows, LANES), jnp.float32)
                    for j in range(PLACES):
                        mean = full[:, 2 * j : 2 * j + 1]
                        var = full[:, 2 * j + 1 : 2 * j + 2] - mean * mean
                        both = jnp.where(lane == 2 * j, mean, both)
                        both = jnp.where(lane == 2 * j + 1, lax.rsqrt(var + 1e-05), both)
                    marks[way] = both

                @pl.when(hops > 0)
                def _():
                    pass_marks(way).wait_recv()

                @pl.when(hops < last)
                def _():
                    pass_marks(way).start()

            @pl.when((hops > 0) & (phase == place))
            def _():
                give_back(way, q).start()

            @pl.when((phase >= 2) & (q == 0))
            def _():
                pl.semaphore_wait(free_sems.at[way], 1)

            lane = lax.broadcasted_iota(jnp.int32, (rows, LANES), 1)
            at = columns(q)
            both = marks[way]
            mean = jnp.sum(jnp.where(lane == 2 * phase, both, 0.0), axis=1, keepdims=True)
            rstd = jnp.sum(jnp.where(lane == 2 * phase + 1, both, 0.0), axis=1, keepdims=True)
            values = line[way, phase, :, at].astype(jnp.float32)
            rows_of[phase % 2, way, core, :, at] = (
                (values - mean) * rstd * gain_ref[:, at] + bias_ref[:, at]
            ).astype(jnp.bfloat16)
            share(way, i).start()

    def project(way, n):
        d = n - LAG * hops_of(way) - PIECES
        phase, tile = d // PIECES, d % PIECES

        @pl.when((d >= 0) & (d < pieces))
        def _():
            @pl.when(tile == 0)
            def _():
                def arrived(q, carry):
                    share(way, phase * PIECES + q).wait_recv()
                    return carry

                lax.fori_loop(0, PIECES, arrived, 0)

            away = tile < tiles
            column = jnp.where(
                away,
                (1 - narrow_at) * half + tile * tile_cols,
                narrow_at * half + (tile - tiles) * tile_cols,
            )
            product = lax.dot_general(
                rows_of[phase % 2, way].reshape(tile_rows, depth),
                weight[:, pl.ds(pl.multiple_of(column, tile_cols), tile_cols)],
                (((1,), (0,)), ((), ())),
                preferred_element_type=jnp.float32,
            ).astype(jnp.bfloat16)

            @pl.when(away)
            def _():
                sending[way, phase, tile] = product
                swap(way, phase, tile).start()

            @pl.when(tile >= tiles)
            def _():
                for which in range(2):
                    at = pl.ds((2 * which + way) * rows, rows)
                    joined[phase, at, tile_at(tile - tiles)] = product[which * rows : (which + 1) * rows]

            @pl.when((tile == PIECES - 1) & (phase < PLACES - 2))
            def _():
                pl.semaphore_signal(free_sems.at[way], inc=1, device_id=twin, device_id_type=MESH)

        t = d - tiles - TAKE_LAG
        taken, of = t // PIECES, t % PIECES

        @pl.when((t >= 0) & (t < pieces) & (of < tiles))
        def _():
            swap(way, taken, of).wait()
            for which in range(2):
                at = pl.ds((2 * which + way) * rows, rows)
                came = coming[way, taken, of, which * rows : (which + 1) * rows].astype(jnp.float32)
                both = joined[taken, at, tile_at(of)].astype(jnp.float32) + came
                joined[taken, at, tile_at(of)] = both.astype(jnp.bfloat16)

    whole = LAG * jnp.maximum(place, last - place) + PIECES + 2 * tiles + TAKE_LAG

    def tick(n, carry):
        for way in range(2):
            arrive(way, n)

        @pl.when(n == PIECES)
        def _():
            fetch.wait()

        for way in range(2):
            project(way, n)

        a = n - whole
        head = a % PIECES
        for block in range(PLACES):

            @pl.when((a // PIECES == block) & (head < heads) & (a >= 0))
            def _():
                attended[block, head] = attend_block(joined, head, block)

                @pl.when(narrow_at == block // 2)
                def _():
                    keep(block, head).start()

                if block >= PLACES // 2:

                    @pl.when(narrow_at != block // 2)
                    def _():
                        deliver(block, head).start()

        @pl.when((n == LAG * last + pieces + tiles) & (narrow_at == 1))
        def _():
            for block in range(PLACES // 2):
                for head in range(heads):
                    deliver(block, head).start()

        return carry

    lax.fori_loop(0, LAG * last + PIECES + 2 * tiles + TAKE_LAG + (PLACES - 1) * PIECES + heads, tick, 0)

    for way in range(2):

        @pl.when(hops_of(way) < last)
        def _():
            pass_marks(way).wait_send()

        @pl.when(hops_of(way) > 0)
        def _():
            for q in range(PIECES):
                give_back(way, q).wait()

        @pl.when(at_source(way))
        def _():
            settle(way).wait()

    for block in range(2):
        for head in range(heads):
            deliver(block, head).wait()
            keep(block, head).wait()


def qkv_rows(raw, marks, own, gain, bias, qkv_weight):
    rows, depth = raw.shape[1:]
    width = qkv_weight.shape[1]
    half = width // 2
    tiles = PIECES // 2
    heads = half // (3 * HDIM)
    passed = (2, PLACES, tiles, 2 * rows, half // tiles)
    pieces = PLACES * PIECES
    seq_len = 4 * PLACES * rows
    vmem = pl.BlockSpec(memory_space=pltpu.VMEM)
    hbm = pl.BlockSpec(memory_space=pl.ANY)
    return pl.pallas_call(
        qkv_attend,
        in_specs=[hbm, vmem, hbm, vmem, vmem, hbm],
        out_specs=[hbm, hbm],
        out_shape=[
            jax.ShapeDtypeStruct((seq_len // 2, 2 * heads * HDIM), jnp.bfloat16),
            jax.ShapeDtypeStruct((2 * rows, depth), jnp.bfloat16),
        ],
        scratch_shapes=[
            pltpu.VMEM((2, PLACES, rows, depth), jnp.bfloat16),
            pltpu.VMEM((2, rows, LANES), jnp.float32),
            pltpu.VMEM((2, rows, LANES), jnp.float32),
            pltpu.VMEM((2, 2, 2, rows, depth), jnp.bfloat16),
            pltpu.VMEM((depth, width), jnp.bfloat16),
            pltpu.VMEM(passed, jnp.bfloat16),
            pltpu.VMEM(passed, jnp.bfloat16),
            pltpu.VMEM((PLACES, 4 * rows, half), jnp.bfloat16),
            pltpu.VMEM((PLACES, heads, 4 * rows, HDIM), jnp.bfloat16),
            pltpu.SemaphoreType.DMA((2,)),
            pltpu.SemaphoreType.DMA,
            pltpu.SemaphoreType.DMA((PLACES,)),
            pltpu.SemaphoreType.DMA,
            pltpu.SemaphoreType.DMA((2, 2)),
            pltpu.SemaphoreType.DMA((2, 2, pieces)),
            pltpu.SemaphoreType.DMA((2, 2, pieces)),
            pltpu.SemaphoreType.DMA((2, 2, PIECES)),
            pltpu.SemaphoreType.DMA((2, 2, PLACES, tiles)),
            pltpu.SemaphoreType.DMA((3, 2, heads)),
            pltpu.SemaphoreType.REGULAR((2,)),
        ],
        compiler_params=pltpu.CompilerParams(
            collective_id=1, has_side_effects=True, vmem_limit_bytes=63 << 20
        ),
        cost_estimate=pl.CostEstimate(
            flops=2 * seq_len * depth * width + 3 * heads * seq_len * seq_len * HDIM,
            bytes_accessed=2 * depth * width,
            transcendentals=heads * seq_len * seq_len // 2,
        ),
    )(raw, marks, own, gain, bias, qkv_weight)


def copy_both(attended_hbm, mine_hbm, out_hbm, stream_hbm, attended, mine, sems):
    steps = []
    pairs = ((mine_hbm, mine, stream_hbm), (attended_hbm, attended, out_hbm))
    for which, (source, held, target) in enumerate(pairs):
        rows = source.shape[0] // COPIES
        for part in range(COPIES):
            at = pl.ds(part * rows, rows)
            load = pltpu.make_async_copy(source.at[at], held.at[at], sems.at[0, which, part])
            store = pltpu.make_async_copy(held.at[at], target.at[at], sems.at[1, which, part])
            steps.append((load, store))
    for load, _ in steps:
        load.start()
    for load, store in steps:
        load.wait()
        store.start()
    for _, store in steps:
        store.wait()


def hand_over(attended, mine):
    hbm = pl.BlockSpec(memory_space=pl.ANY)
    return pl.pallas_call(
        copy_both,
        in_specs=[hbm, hbm],
        out_specs=[hbm, hbm],
        out_shape=[jax.ShapeDtypeStruct(a.shape, a.dtype) for a in (attended, mine)],
        scratch_shapes=[
            pltpu.VMEM(attended.shape, attended.dtype),
            pltpu.VMEM(mine.shape, mine.dtype),
            pltpu.SemaphoreType.DMA((2, 2, COPIES)),
        ],
        compiler_params=pltpu.CompilerParams(vmem_limit_bytes=62 << 20),
    )(attended, mine)


def split_heads(hidden, down_weight, residual, ln_gain, ln_bias, qkv_weight):
    own, raw, marks = ffn_rows(hidden[0], down_weight, residual[0])
    attended, mine = qkv_rows(raw, marks, own, ln_gain[None], ln_bias[None], qkv_weight)
    attended, mine = hand_over(attended, mine)
    return (mine[None], attended[None])


def split_queries(hidden, down_weight, residual, ln_gain, ln_bias, qkv_weight):
    inner = hidden[0]
    resid = residual[0]
    seq_len = inner.shape[0]
    wide_rows = seq_len // lax.axis_size("wide")
    wide_at = lax.axis_index("wide")
    contract = (((1,), (1,)), ((), ()))
    partial_ffn = lax.dot_general(inner, down_weight, contract, preferred_element_type=jnp.float32)
    summed = lax.psum(partial_ffn, "wide")
    mine = (resid.astype(jnp.float32) + summed).astype(jnp.bfloat16)
    arrived = from_behind(mine, "section", 1)
    own_rows = lax.dynamic_slice_in_dim(mine, wide_at * wide_rows, wide_rows, 0)
    values = arrived.astype(jnp.float32)
    totals, squares = lax.psum(
        (jnp.sum(values, axis=1), jnp.sum(values * values, axis=1)), "narrow"
    )
    mean = totals / D
    var = squares / D - mean * mean
    normed = (
        (values - mean[:, None]) * lax.rsqrt(var + 1e-05)[:, None] * ln_gain + ln_bias
    ).astype(jnp.bfloat16)
    heads_here = qkv_weight.shape[1] // (3 * HDIM)
    query_count = seq_len // lax.axis_size("narrow")
    narrow_at = lax.axis_index("narrow")
    joined = lax.psum(
        jnp.dot(normed, qkv_weight, preferred_element_type=jnp.float32), "narrow"
    ).astype(jnp.bfloat16)
    mine_joined = lax.dynamic_slice_in_dim(joined, narrow_at * query_count, query_count, 0)
    query = mine_joined.reshape(query_count, heads_here, 3, HDIM)[:, :, 0]
    pairs = joined.reshape(seq_len, heads_here, 3, HDIM)[:, :, 1:]
    keys = pairs[:, :, 0]
    vals = pairs[:, :, 1]
    scores = jnp.einsum("qhd,khd->hqk", query, keys, preferred_element_type=jnp.float32) / jnp.sqrt(
        jnp.float32(HDIM)
    )
    query_pos = narrow_at * query_count + lax.broadcasted_iota(jnp.int32, (query_count, seq_len), 0)
    key_pos = lax.broadcasted_iota(jnp.int32, (query_count, seq_len), 1)
    scores = jnp.where((key_pos <= query_pos)[None], scores, jnp.float32(-1e30))
    top = jnp.max(scores, axis=2, keepdims=True)
    expd = jnp.exp(scores - top)
    probs = (expd / jnp.sum(expd, axis=2, keepdims=True)).astype(jnp.bfloat16)
    attended = jnp.einsum("hqk,khd->qhd", probs, vals, preferred_element_type=jnp.float32).astype(
        jnp.bfloat16
    )
    attended = attended.reshape(query_count, heads_here * HDIM)
    return (own_rows[None], attended[None])


def per_device(hidden, down_weight, residual, ln_gain, ln_bias, qkv_weight):
    heads_here = qkv_weight.shape[1] // (3 * HDIM)
    wide_rows = hidden.shape[1] // lax.axis_size("wide")
    even = heads_here % 8 == 0 and wide_rows % 32 == 0
    line = lax.axis_size("section") == 2 and lax.axis_size("wide") == 2 * PLACES and lax.axis_size("narrow") == 2
    even = even and down_weight.shape[0] % (FFN_STEPS * 128) == 0
    plan = split_heads if line and even else split_queries
    return plan(hidden, down_weight, residual, ln_gain, ln_bias, qkv_weight)


def solution(mesh):
    return jax.shard_map(
        per_device,
        mesh=mesh,
        in_specs=(
            P("section", None, "wide"),
            P("narrow", "wide"),
            P("section", None, "narrow"),
            P("narrow"),
            P("narrow"),
            P("narrow", "wide"),
        ),
        out_specs=(P("section", "wide", "narrow"), P("section", "narrow", "wide")),
        check_vma=False,
    )
```

```python
import functools

import jax
import jax.numpy as jnp
from jax import lax
from jax.experimental import pallas as pl
from jax.experimental.pallas import tpu as pltpu
from jax.sharding import PartitionSpec as P

D = 12288
HDIM = 128
LANES = 128
PLACES = 4
FFN_STEPS = 24
PIECES = 6
LAG = 2
TAKE_LAG = 3
SENT_LAG = 2
SWAP_LAG = 3
COPIES = 4
MESH = pl.DeviceIdType.MESH


def from_behind(value, axis, steps):
    count = lax.axis_size(axis)
    pairs = [(source, (source + steps) % count) for source in range(count)]
    return lax.ppermute(value, axis, pairs)


def attend_block(joined_ref, head, block):
    factor = 1.4426950408889634 / (HDIM**0.5)
    size = joined_ref.shape[1]

    def part(which):
        return pl.ds(pl.multiple_of((3 * head + which) * HDIM, HDIM), HDIM)

    def scores_of(keys):
        return lax.dot_general(query, keys, (((1,), (1,)), ((), ())), preferred_element_type=jnp.float32)

    query = joined_ref[block, :, part(0)]
    shape = (size, size)
    seen = lax.broadcasted_iota(jnp.int32, shape, 1) <= lax.broadcasted_iota(jnp.int32, shape, 0)
    near = jnp.where(seen, scores_of(joined_ref[block, :, part(1)]), jnp.float32(-1e30))
    top = jnp.max(near, axis=1, keepdims=True)
    if block:
        far = scores_of(joined_ref[:block, :, part(1)].reshape(block * size, HDIM))
        top = jnp.maximum(top, jnp.max(far, axis=1, keepdims=True))
    near = jnp.exp2((near - top) * factor)
    total = jnp.sum(near, axis=1, keepdims=True)
    out = jnp.dot(
        near.astype(jnp.bfloat16), joined_ref[block, :, part(2)], preferred_element_type=jnp.float32
    )
    if block:
        far = jnp.exp2((far - top) * factor)
        total += jnp.sum(far, axis=1, keepdims=True)
        out += jnp.dot(
            far.astype(jnp.bfloat16),
            joined_ref[:block, :, part(2)].reshape(block * size, HDIM),
            preferred_element_type=jnp.float32,
        )
    return (out * (1.0 / total)).astype(jnp.bfloat16)


def greet(place, core, others):
    barrier = pltpu.get_barrier_semaphore()
    pl.semaphore_signal(barrier, inc=1, device_id={"wide": place * 2 + 1 - core}, device_id_type=MESH)
    for other in others:
        pl.semaphore_signal(barrier, inc=1, device_id=other, device_id_type=MESH)

    @pl.when(place > 0)
    def _():
        pl.semaphore_signal(
            barrier, inc=1, device_id={"wide": (place - 1) * 2 + core}, device_id_type=MESH
        )

    @pl.when(place < PLACES - 1)
    def _():
        pl.semaphore_signal(
            barrier, inc=1, device_id={"wide": (place + 1) * 2 + core}, device_id_type=MESH
        )


def await_greetings(place, count):
    barrier = pltpu.get_barrier_semaphore()

    @pl.when((place == 0) | (place == PLACES - 1))
    def _():
        pl.semaphore_wait(barrier, count)

    @pl.when((place > 0) & (place < PLACES - 1))
    def _():
        pl.semaphore_wait(barrier, count + 1)


def ffn_ends(
    steps, hidden_ref, weight_ref, resid_hbm, own_hbm, raw_hbm, sums_ref,
    sums, swapped, line, resid, stream, acc, parts,
    swap_sems, line_sems, cross_sems, own_sems, resid_sem, part_sems,
):
    wide_at = lax.axis_index("wide")
    section_at = lax.axis_index("section")
    place, core = wide_at // 2, wide_at % 2
    step = pl.program_id(0)
    rows, cols = sums.shape[4], sums.shape[5]
    last = PLACES - 1
    at_end = (place == 0) | (place == last)
    across = {"section": 1 - section_at}

    def fetch(kept):
        return pltpu.make_async_copy(resid_hbm.at[:, core, kept], resid, resid_sem)

    @pl.when(step == 0)
    def _():
        @pl.when(place == 0)
        def _():
            fetch(1).start()

        @pl.when(place == last)
        def _():
            fetch(0).start()

        greet(place, core, (across,))
        acc[...] = jnp.zeros_like(acc)

    def swap(i):
        return pltpu.make_async_remote_copy(
            src_ref=sums.at[i, 1 - core],
            dst_ref=swapped.at[i],
            send_sem=swap_sems.at[0, i],
            recv_sem=swap_sems.at[1, i],
            device_id={"wide": place * 2 + 1 - core},
            device_id_type=MESH,
        )

    def pass_on(way, i):
        towards = place + 1 if way == 0 else place - 1
        return pltpu.make_async_remote_copy(
            src_ref=line.at[way, i],
            dst_ref=line.at[way, i],
            send_sem=line_sems.at[way, 0, i],
            recv_sem=line_sems.at[way, 1, i],
            device_id={"wide": towards * 2 + core},
            device_id_type=MESH,
        )

    def columns(i):
        return pl.ds(pl.multiple_of(i * cols, cols), cols)

    def cross(i):
        return pltpu.make_async_remote_copy(
            src_ref=stream.at[:, :, columns(i)],
            dst_ref=raw_hbm.at[:, :, columns(i)],
            send_sem=cross_sems.at[0, i],
            recv_sem=cross_sems.at[1, i],
            device_id=across,
            device_id_type=MESH,
        )

    def store(i):
        return pltpu.make_async_copy(
            stream.at[place, :, columns(i)], own_hbm.at[:, columns(i)], own_sems.at[i]
        )

    @pl.when(step < steps)
    def _():
        result = lax.dot_general(
            hidden_ref[...], weight_ref[...], (((1,), (1,)), ((), ())), preferred_element_type=jnp.float32
        ).astype(jnp.bfloat16)
        for j in range(PLACES):
            part = result[4 * rows * j : 4 * rows * (j + 1)]
            sums[step, :, :, j] = part.reshape(2, 2, rows, cols)

        @pl.when(step == 0)
        def _():
            await_greetings(place, 3)

        swap(step).start()

    @pl.when((step >= SWAP_LAG) & (step < steps + SWAP_LAG))
    def _():
        swap(step - SWAP_LAG).wait_send()

    for way in range(2):
        hops = place if way == 0 else last - place
        i = step - 1 - LAG * hops
        live = (i >= 0) & (i < steps)

        def mine(j):
            return sums[i, core, way, j].astype(jnp.float32) + swapped[i, way, j].astype(jnp.float32)

        sent = i - SENT_LAG

        @pl.when((sent >= 0) & (sent < steps) & (hops < last))
        def _():
            pass_on(way, sent).wait_send()

        @pl.when((sent >= 0) & (hops == last))
        def _():
            cross(sent).wait()
            store(sent).wait()

        @pl.when(live & (hops < last - hops))
        def _():
            swap(i).wait_recv()

        @pl.when(live & (hops > 0))
        def _():
            pass_on(way, i).wait_recv()

        @pl.when(live & (hops == 0))
        def _():
            for j in range(PLACES):
                line[way, i, j] = mine(j).astype(jnp.bfloat16)

        @pl.when(live & (hops > 0) & (hops < last))
        def _():
            for j in range(PLACES):
                line[way, i, j] = (mine(j) + line[way, i, j].astype(jnp.float32)).astype(jnp.bfloat16)

        @pl.when(live & (hops < last))
        def _():
            pass_on(way, i).start()

        @pl.when(live & (hops == last))
        def _():
            @pl.when(i == 0)
            def _():
                fetch(way).wait()

            for j in range(PLACES):
                total = mine(j) + line[way, i, j].astype(jnp.float32)
                rounded = (resid[j, :, columns(i)].astype(jnp.float32) + total).astype(jnp.bfloat16)
                stream[j, :, columns(i)] = rounded
                values = rounded.astype(jnp.float32)
                for at in range(0, cols, LANES):
                    piece = values[:, at : at + LANES]
                    acc[0, j] += piece
                    acc[1, j] += piece * piece
            cross(i).start()
            store(i).start()

    @pl.when(step == steps + LAG * last)
    def _():
        @pl.when(at_end)
        def _():
            lane = lax.broadcasted_iota(jnp.int32, (rows, LANES), 1)
            packed = jnp.zeros((rows, LANES), jnp.float32)
            for j in range(PLACES):
                for which in range(2):
                    total = jnp.sum(acc[which, j], axis=1, keepdims=True)
                    packed = jnp.where(lane == 2 * j + which, total, packed)
            parts[0] = packed
            give = pltpu.make_async_remote_copy(
                src_ref=parts.at[0],
                dst_ref=parts.at[1],
                send_sem=part_sems.at[0],
                recv_sem=part_sems.at[1],
                device_id=across,
                device_id_type=MESH,
            )
            give.start()
            give.wait()
            sums_ref[...] = parts[1]

        @pl.when(at_end)
        def _():
            for i in range(steps - SENT_LAG, steps):
                cross(i).wait()
                store(i).wait()


def ffn_rows(inner, down_weight, residual):
    seq_len, units = inner.shape
    width = down_weight.shape[0]
    cols = width // FFN_STEPS
    rows = seq_len // (4 * PLACES)
    last_step = FFN_STEPS - 1
    return pl.pallas_call(
        functools.partial(ffn_ends, FFN_STEPS),
        grid=(FFN_STEPS + LAG * (PLACES - 1) + 1,),
        in_specs=[
            pl.BlockSpec((seq_len, units), lambda s: (0, 0), pipeline_mode=pl.Buffered(1)),
            pl.BlockSpec((cols, units), lambda s: (jnp.minimum(s, last_step), 0)),
            pl.BlockSpec(memory_space=pl.ANY),
        ],
        out_specs=[
            pl.BlockSpec(memory_space=pl.ANY),
            pl.BlockSpec(memory_space=pl.ANY),
            pl.BlockSpec((rows, LANES), lambda s: (0, 0), pipeline_mode=pl.Buffered(1)),
        ],
        out_shape=[
            jax.ShapeDtypeStruct((rows, width), jnp.bfloat16),
            jax.ShapeDtypeStruct((PLACES, rows, width), jnp.bfloat16),
            jax.ShapeDtypeStruct((rows, LANES), jnp.float32),
        ],
        scratch_shapes=[
            pltpu.VMEM((FFN_STEPS, 2, 2, PLACES, rows, cols), jnp.bfloat16),
            pltpu.VMEM((FFN_STEPS, 2, PLACES, rows, cols), jnp.bfloat16),
            pltpu.VMEM((2, FFN_STEPS, PLACES, rows, cols), jnp.bfloat16),
            pltpu.VMEM((PLACES, rows, width), jnp.bfloat16),
            pltpu.VMEM((PLACES, rows, width), jnp.bfloat16),
            pltpu.VMEM((2, PLACES, rows, LANES), jnp.float32),
            pltpu.VMEM((2, rows, LANES), jnp.float32),
            pltpu.SemaphoreType.DMA((2, FFN_STEPS)),
            pltpu.SemaphoreType.DMA((2, 2, FFN_STEPS)),
            pltpu.SemaphoreType.DMA((2, FFN_STEPS)),
            pltpu.SemaphoreType.DMA((FFN_STEPS,)),
            pltpu.SemaphoreType.DMA,
            pltpu.SemaphoreType.DMA((2,)),
        ],
        compiler_params=pltpu.CompilerParams(
            collective_id=0, has_side_effects=True, vmem_limit_bytes=60 << 20
        ),
        cost_estimate=pl.CostEstimate(
            flops=2 * seq_len * units * width, bytes_accessed=2 * units * width, transcendentals=0
        ),
    )(inner, down_weight, residual.reshape(PLACES, 2, 2, rows, width))


def qkv_attend(
    raw_hbm, sums_in, own_hbm, gain_ref, bias_ref, weight_hbm, out_hbm, mine_hbm,
    line, marks, parts, rows_of, weight, sending, coming, joined, attended,
    part_sems, weight_sem, raw_sems, own_sem, mark_sems, line_sems, share_sems, back_sems, swap_sems, out_sems,
    free_sems,
):
    wide_at = lax.axis_index("wide")
    section_at = lax.axis_index("section")
    narrow_at = lax.axis_index("narrow")
    place, core = wide_at // 2, wide_at % 2
    last = PLACES - 1
    tiles, tile_rows, tile_cols = sending.shape[2:]
    half = tiles * tile_cols
    rows, depth = rows_of.shape[3:]
    cols = depth // PIECES
    pieces = PLACES * PIECES
    heads = attended.shape[1]
    across = {"section": 1 - section_at}
    partner = {"narrow": 1 - narrow_at}
    twin = {"wide": place * 2 + 1 - core}

    fetch = pltpu.make_async_copy(weight_hbm, weight, weight_sem)

    def begin(kept, j):
        return pltpu.make_async_copy(raw_hbm.at[j], line.at[kept, j], raw_sems.at[j])

    def settle(kept):
        return pltpu.make_async_copy(own_hbm, mine_hbm.at[pl.ds(kept * rows, rows)], own_sem)

    def at_source(kept):
        return place == (last if kept == 0 else 0)

    for kept in range(2):

        @pl.when(at_source(kept))
        def _():
            for j in range(PLACES):
                begin(kept, j).start()
            parts[0] = sums_in[...]

    fetch.start()
    greet(place, core, (across, partner))
    await_greetings(place, 4)
    add_up = pltpu.make_async_remote_copy(
        src_ref=parts.at[0],
        dst_ref=parts.at[1],
        send_sem=part_sems.at[0],
        recv_sem=part_sems.at[1],
        device_id=partner,
        device_id_type=MESH,
    )
    for kept in range(2):

        @pl.when(at_source(kept))
        def _():
            add_up.start()
            settle(kept).start()

    def onwards(way):
        return {"wide": (place - 1 if way == 0 else place + 1) * 2 + core}

    def columns(q):
        return pl.ds(pl.multiple_of(q * cols, cols), cols)

    def pass_marks(way):
        return pltpu.make_async_remote_copy(
            src_ref=marks.at[way],
            dst_ref=marks.at[way],
            send_sem=mark_sems.at[way, 0],
            recv_sem=mark_sems.at[way, 1],
            device_id=onwards(way),
            device_id_type=MESH,
        )

    def pass_on(way, i):
        part = line.at[way, i // PIECES, :, columns(i % PIECES)]
        return pltpu.make_async_remote_copy(
            src_ref=part,
            dst_ref=part,
            send_sem=line_sems.at[way, 0, i],
            recv_sem=line_sems.at[way, 1, i],
            device_id=onwards(way),
            device_id_type=MESH,
        )

    def give_back(way, q):
        return pltpu.make_async_remote_copy(
            src_ref=line.at[way, place, :, columns(q)],
            dst_ref=mine_hbm.at[pl.ds(way * rows, rows), columns(q)],
            send_sem=back_sems.at[way, 0, q],
            recv_sem=back_sems.at[way, 1, q],
            device_id=across,
            device_id_type=MESH,
        )

    def share(way, i):
        part = rows_of.at[(i // PIECES) % 2, way, core, :, columns(i % PIECES)]
        return pltpu.make_async_remote_copy(
            src_ref=part,
            dst_ref=part,
            send_sem=share_sems.at[way, 0, i],
            recv_sem=share_sems.at[way, 1, i],
            device_id=twin,
            device_id_type=MESH,
        )

    def swap(way, phase, tile):
        return pltpu.make_async_remote_copy(
            src_ref=sending.at[way, phase, tile],
            dst_ref=coming.at[way, phase, tile],
            send_sem=swap_sems.at[way, 0, phase, tile],
            recv_sem=swap_sems.at[way, 1, phase, tile],
            device_id=partner,
            device_id_type=MESH,
        )

    def into(block, head):
        row = pl.ds((block % 2) * 4 * rows, 4 * rows)
        column = pl.ds(pl.multiple_of((narrow_at * heads + head) * HDIM, HDIM), HDIM)
        return out_hbm.at[row, column]

    def deliver(block, head):
        return pltpu.make_async_remote_copy(
            src_ref=attended.at[block, head],
            dst_ref=into(block, head),
            send_sem=out_sems.at[0, block % 2, head],
            recv_sem=out_sems.at[1, block % 2, head],
            device_id=partner,
            device_id_type=MESH,
        )

    def keep(block, head):
        return pltpu.make_async_copy(
            attended.at[block, head], into(block, head), out_sems.at[2, block % 2, head]
        )

    def hops_of(way):
        return last - place if way == 0 else place

    def tile_at(tile):
        return pl.ds(pl.multiple_of(tile * tile_cols, tile_cols), tile_cols)

    def arrive(way, n):
        hops = hops_of(way)
        i = n - LAG * hops
        phase, q = i // PIECES, i % PIECES
        sent = i - SENT_LAG

        @pl.when((sent >= 0) & (sent < pieces))
        def _():
            share(way, sent).wait_send()

            @pl.when(hops < last)
            def _():
                pass_on(way, sent).wait_send()

        @pl.when((i >= 0) & (i < pieces))
        def _():
            @pl.when((hops == 0) & (q == 0))
            def _():
                begin(way, phase).wait()

            @pl.when(hops > 0)
            def _():
                pass_on(way, i).wait_recv()

            @pl.when(hops < last)
            def _():
                pass_on(way, i).start()

            @pl.when(i == 0)
            def _():
                @pl.when(hops == 0)
                def _():
                    add_up.wait()
                    full = (parts[0] + parts[1]) / D
                    lane = lax.broadcasted_iota(jnp.int32, (rows, LANES), 1)
                    both = jnp.zeros((rows, LANES), jnp.float32)
                    for j in range(PLACES):
                        mean = full[:, 2 * j : 2 * j + 1]
                        var = full[:, 2 * j + 1 : 2 * j + 2] - mean * mean
                        both = jnp.where(lane == 2 * j, mean, both)
                        both = jnp.where(lane == 2 * j + 1, lax.rsqrt(var + 1e-05), both)
                    marks[way] = both

                @pl.when(hops > 0)
                def _():
                    pass_marks(way).wait_recv()

                @pl.when(hops < last)
                def _():
                    pass_marks(way).start()

            @pl.when((hops > 0) & (phase == place))
            def _():
                give_back(way, q).start()

            @pl.when((phase >= 2) & (q == 0))
            def _():
                pl.semaphore_wait(free_sems.at[way], 1)

            lane = lax.broadcasted_iota(jnp.int32, (rows, LANES), 1)
            at = columns(q)
            both = marks[way]
            mean = jnp.sum(jnp.where(lane == 2 * phase, both, 0.0), axis=1, keepdims=True)
            rstd = jnp.sum(jnp.where(lane == 2 * phase + 1, both, 0.0), axis=1, keepdims=True)
            values = line[way, phase, :, at].astype(jnp.float32)
            rows_of[phase % 2, way, core, :, at] = (
                (values - mean) * rstd * gain_ref[:, at] + bias_ref[:, at]
            ).astype(jnp.bfloat16)
            share(way, i).start()

    def project(way, n):
        d = n - LAG * hops_of(way) - PIECES
        phase, tile = d // PIECES, d % PIECES

        @pl.when((d >= 0) & (d < pieces))
        def _():
            @pl.when(tile == 0)
            def _():
                def arrived(q, carry):
                    share(way, phase * PIECES + q).wait_recv()
                    return carry

                lax.fori_loop(0, PIECES, arrived, 0)

            away = tile < tiles
            column = jnp.where(
                away,
                (1 - narrow_at) * half + tile * tile_cols,
                narrow_at * half + (tile - tiles) * tile_cols,
            )
            product = lax.dot_general(
                rows_of[phase % 2, way].reshape(tile_rows, depth),
                weight[:, pl.ds(pl.multiple_of(column, tile_cols), tile_cols)],
                (((1,), (0,)), ((), ())),
                preferred_element_type=jnp.float32,
            ).astype(jnp.bfloat16)

            @pl.when(away)
            def _():
                sending[way, phase, tile] = product
                swap(way, phase, tile).start()

            @pl.when(tile >= tiles)
            def _():
                for which in range(2):
                    at = pl.ds((2 * which + way) * rows, rows)
                    joined[phase, at, tile_at(tile - tiles)] = product[which * rows : (which + 1) * rows]

            @pl.when((tile == PIECES - 1) & (phase < PLACES - 2))
            def _():
                pl.semaphore_signal(free_sems.at[way], inc=1, device_id=twin, device_id_type=MESH)

        t = d - tiles - TAKE_LAG
        taken, of = t // PIECES, t % PIECES

        @pl.when((t >= 0) & (t < pieces) & (of < tiles))
        def _():
            swap(way, taken, of).wait()
            for which in range(2):
                at = pl.ds((2 * which + way) * rows, rows)
                came = coming[way, taken, of, which * rows : (which + 1) * rows].astype(jnp.float32)
                both = joined[taken, at, tile_at(of)].astype(jnp.float32) + came
                joined[taken, at, tile_at(of)] = both.astype(jnp.bfloat16)

    whole = LAG * jnp.maximum(place, last - place) + PIECES + 2 * tiles + TAKE_LAG

    def tick(n, carry):
        for way in range(2):
            arrive(way, n)

        @pl.when(n == PIECES)
        def _():
            fetch.wait()

        for way in range(2):
            project(way, n)

        a = n - whole
        head = a % PIECES
        for block in range(PLACES):

            @pl.when((a // PIECES == block) & (head < heads) & (a >= 0))
            def _():
                attended[block, head] = attend_block(joined, head, block)

                @pl.when(narrow_at == block // 2)
                def _():
                    keep(block, head).start()

                if block >= PLACES // 2:

                    @pl.when(narrow_at != block // 2)
                    def _():
                        deliver(block, head).start()

        @pl.when((n == LAG * last + pieces + tiles) & (narrow_at == 1))
        def _():
            for block in range(PLACES // 2):
                for head in range(heads):
                    deliver(block, head).start()

        return carry

    lax.fori_loop(0, LAG * last + PIECES + 2 * tiles + TAKE_LAG + (PLACES - 1) * PIECES + heads, tick, 0)

    for way in range(2):

        @pl.when(hops_of(way) < last)
        def _():
            pass_marks(way).wait_send()

        @pl.when(hops_of(way) > 0)
        def _():
            for q in range(PIECES):
                give_back(way, q).wait()

        @pl.when(at_source(way))
        def _():
            settle(way).wait()

    for block in range(2):
        for head in range(heads):
            deliver(block, head).wait()
            keep(block, head).wait()


def qkv_rows(raw, marks, own, gain, bias, qkv_weight):
    rows, depth = raw.shape[1:]
    width = qkv_weight.shape[1]
    half = width // 2
    tiles = PIECES // 2
    heads = half // (3 * HDIM)
    passed = (2, PLACES, tiles, 2 * rows, half // tiles)
    pieces = PLACES * PIECES
    seq_len = 4 * PLACES * rows
    vmem = pl.BlockSpec(memory_space=pltpu.VMEM)
    hbm = pl.BlockSpec(memory_space=pl.ANY)
    return pl.pallas_call(
        qkv_attend,
        in_specs=[hbm, vmem, hbm, vmem, vmem, hbm],
        out_specs=[hbm, hbm],
        out_shape=[
            jax.ShapeDtypeStruct((seq_len // 2, 2 * heads * HDIM), jnp.bfloat16),
            jax.ShapeDtypeStruct((2 * rows, depth), jnp.bfloat16),
        ],
        scratch_shapes=[
            pltpu.VMEM((2, PLACES, rows, depth), jnp.bfloat16),
            pltpu.VMEM((2, rows, LANES), jnp.float32),
            pltpu.VMEM((2, rows, LANES), jnp.float32),
            pltpu.VMEM((2, 2, 2, rows, depth), jnp.bfloat16),
            pltpu.VMEM((depth, width), jnp.bfloat16),
            pltpu.VMEM(passed, jnp.bfloat16),
            pltpu.VMEM(passed, jnp.bfloat16),
            pltpu.VMEM((PLACES, 4 * rows, half), jnp.bfloat16),
            pltpu.VMEM((PLACES, heads, 4 * rows, HDIM), jnp.bfloat16),
            pltpu.SemaphoreType.DMA((2,)),
            pltpu.SemaphoreType.DMA,
            pltpu.SemaphoreType.DMA((PLACES,)),
            pltpu.SemaphoreType.DMA,
            pltpu.SemaphoreType.DMA((2, 2)),
            pltpu.SemaphoreType.DMA((2, 2, pieces)),
            pltpu.SemaphoreType.DMA((2, 2, pieces)),
            pltpu.SemaphoreType.DMA((2, 2, PIECES)),
            pltpu.SemaphoreType.DMA((2, 2, PLACES, tiles)),
            pltpu.SemaphoreType.DMA((3, 2, heads)),
            pltpu.SemaphoreType.REGULAR((2,)),
        ],
        compiler_params=pltpu.CompilerParams(
            collective_id=1, has_side_effects=True, vmem_limit_bytes=63 << 20
        ),
        cost_estimate=pl.CostEstimate(
            flops=2 * seq_len * depth * width + 3 * heads * seq_len * seq_len * HDIM,
            bytes_accessed=2 * depth * width,
            transcendentals=heads * seq_len * seq_len // 2,
        ),
    )(raw, marks, own, gain, bias, qkv_weight)


def copy_both(attended_hbm, mine_hbm, out_hbm, stream_hbm, attended, mine, sems):
    steps = []
    pairs = ((mine_hbm, mine, stream_hbm), (attended_hbm, attended, out_hbm))
    for which, (source, held, target) in enumerate(pairs):
        rows = source.shape[0] // COPIES
        for part in range(COPIES):
            at = pl.ds(part * rows, rows)
            load = pltpu.make_async_copy(source.at[at], held.at[at], sems.at[0, which, part])
            store = pltpu.make_async_copy(held.at[at], target.at[at], sems.at[1, which, part])
            steps.append((load, store))
    for load, _ in steps:
        load.start()
    for load, store in steps:
        load.wait()
        store.start()
    for _, store in steps:
        store.wait()


def hand_over(attended, mine):
    hbm = pl.BlockSpec(memory_space=pl.ANY)
    return pl.pallas_call(
        copy_both,
        in_specs=[hbm, hbm],
        out_specs=[hbm, hbm],
        out_shape=[jax.ShapeDtypeStruct(a.shape, a.dtype) for a in (attended, mine)],
        scratch_shapes=[
            pltpu.VMEM(attended.shape, attended.dtype),
            pltpu.VMEM(mine.shape, mine.dtype),
            pltpu.SemaphoreType.DMA((2, 2, COPIES)),
        ],
        compiler_params=pltpu.CompilerParams(vmem_limit_bytes=62 << 20),
    )(attended, mine)


def split_heads(hidden, down_weight, residual, ln_gain, ln_bias, qkv_weight):
    own, raw, marks = ffn_rows(hidden[0], down_weight, residual[0])
    attended, mine = qkv_rows(raw, marks, own, ln_gain[None], ln_bias[None], qkv_weight)
    attended, mine = hand_over(attended, mine)
    return (mine[None], attended[None])


def split_queries(hidden, down_weight, residual, ln_gain, ln_bias, qkv_weight):
    inner = hidden[0]
    resid = residual[0]
    seq_len = inner.shape[0]
    wide_rows = seq_len // lax.axis_size("wide")
    wide_at = lax.axis_index("wide")
    contract = (((1,), (1,)), ((), ()))
    partial_ffn = lax.dot_general(inner, down_weight, contract, preferred_element_type=jnp.float32)
    summed = lax.psum(partial_ffn, "wide")
    mine = (resid.astype(jnp.float32) + summed).astype(jnp.bfloat16)
    arrived = from_behind(mine, "section", 1)
    own_rows = lax.dynamic_slice_in_dim(mine, wide_at * wide_rows, wide_rows, 0)
    values = arrived.astype(jnp.float32)
    totals, squares = lax.psum(
        (jnp.sum(values, axis=1), jnp.sum(values * values, axis=1)), "narrow"
    )
    mean = totals / D
    var = squares / D - mean * mean
    normed = (
        (values - mean[:, None]) * lax.rsqrt(var + 1e-05)[:, None] * ln_gain + ln_bias
    ).astype(jnp.bfloat16)
    heads_here = qkv_weight.shape[1] // (3 * HDIM)
    query_count = seq_len // lax.axis_size("narrow")
    narrow_at = lax.axis_index("narrow")
    joined = lax.psum(
        jnp.dot(normed, qkv_weight, preferred_element_type=jnp.float32), "narrow"
    ).astype(jnp.bfloat16)
    mine_joined = lax.dynamic_slice_in_dim(joined, narrow_at * query_count, query_count, 0)
    query = mine_joined.reshape(query_count, heads_here, 3, HDIM)[:, :, 0]
    pairs = joined.reshape(seq_len, heads_here, 3, HDIM)[:, :, 1:]
    keys = pairs[:, :, 0]
    vals = pairs[:, :, 1]
    scores = jnp.einsum("qhd,khd->hqk", query, keys, preferred_element_type=jnp.float32) / jnp.sqrt(
        jnp.float32(HDIM)
    )
    query_pos = narrow_at * query_count + lax.broadcasted_iota(jnp.int32, (query_count, seq_len), 0)
    key_pos = lax.broadcasted_iota(jnp.int32, (query_count, seq_len), 1)
    scores = jnp.where((key_pos <= query_pos)[None], scores, jnp.float32(-1e30))
    top = jnp.max(scores, axis=2, keepdims=True)
    expd = jnp.exp(scores - top)
    probs = (expd / jnp.sum(expd, axis=2, keepdims=True)).astype(jnp.bfloat16)
    attended = jnp.einsum("hqk,khd->qhd", probs, vals, preferred_element_type=jnp.float32).astype(
        jnp.bfloat16
    )
    attended = attended.reshape(query_count, heads_here * HDIM)
    return (own_rows[None], attended[None])


def per_device(hidden, down_weight, residual, ln_gain, ln_bias, qkv_weight):
    heads_here = qkv_weight.shape[1] // (3 * HDIM)
    wide_rows = hidden.shape[1] // lax.axis_size("wide")
    even = heads_here % 8 == 0 and wide_rows % 32 == 0
    line = lax.axis_size("section") == 2 and lax.axis_size("wide") == 2 * PLACES and lax.axis_size("narrow") == 2
    even = even and down_weight.shape[0] % (FFN_STEPS * 128) == 0
    plan = split_heads if line and even else split_queries
    return plan(hidden, down_weight, residual, ln_gain, ln_bias, qkv_weight)


def solution(mesh):
    return jax.shard_map(
        per_device,
        mesh=mesh,
        in_specs=(
            P("section", None, "wide"),
            P("narrow", "wide"),
            P("section", None, "narrow"),
            P("narrow"),
            P("narrow"),
            P("narrow", "wide"),
        ),
        out_specs=(P("section", "wide", "narrow"), P("section", "narrow", "wide")),
        check_vma=False,
    )
```
